128 devices in a mesh: section: 4 (over x), dp: 32 (over y, z, core).
Axes of the slice: x: 4, y: 4, z: 4, core: 2. Of those that a mesh axis runs over, the one named last changes fastest.
Arguments:
- d_out: bfloat16 [4, 1536, 4096], P('section', 'dp'), may hold values from -6 to 6
- down_weight: bfloat16 [4, 11264, 4096], P('section', 'dp'), may hold values from -0.0546875 to 0.0546875
- gate_weight: bfloat16 [4, 11264, 4096], P('section', 'dp'), may hold values from -0.0546875 to 0.0546875
- up_weight: bfloat16 [4, 11264, 4096], P('section', 'dp'), may hold values from -0.0546875 to 0.0546875
- gate_pre: bfloat16 [4, 1536, 11264], P('section', 'dp'), may hold values from -6 to 6
- up_val: bfloat16 [4, 1536, 11264], P('section', 'dp'), may hold values from -6 to 6
- block_rows: int32 [4, 64], P('section'), may hold values from 0 to 87, as said below
- block_cols: int32 [4, 64], P('section'), may hold values from 0 to 31, as said below
- block_owner: int32 [4, 64], P('section'), may hold values from 0 to 31, as said below
Outputs:
- grad_input: bfloat16 [4, 1536, 4096], P('section', 'dp')
- block_grads: bfloat16 [4, 96, 128, 128], P('section', 'dp')
The draws below stay inside these ranges and needn't reach their ends.
Inputs may be any that keep to these rules, and one draw needn't show every extreme that they name: `block_rows`: the 64 (row, column) pairs of a section are all different. `block_cols`: the 64 (row, column) pairs of a section are all different. `block_owner`: in each section no replica owns more than 3 blocks, and one owns exactly 3.
All inputs are finite; a program needn't handle non-finite values.
Results may differ from the reference program's by a relative error of at most 0.018.
Values may be sent and summed in bfloat16 or wider, within the bound.
A program may use at most 128 MiB of HBM per device.

```python
import jax
import jax.numpy as jnp
from jax import lax

D = 4096
FF = 11264
TOK_DEV = 48
CAP = 3
TOKENS = 1536
NB = 64
N_SECTION = 4
N_DP = 32


def chosen_blocks(key):
    keys = jax.random.split(key, N_SECTION)
    total_blocks = FF // 128 * (D // 128)

    def one_section(section_key):
        return jax.random.permutation(section_key, total_blocks)[:NB].astype(jnp.int32)
    return jax.vmap(one_section)(keys)


def draw_block_rows(key, part):
    picked = chosen_blocks(jax.random.fold_in(key, 11))
    return (picked // (D // 128)).astype(jnp.int32)


def draw_block_cols(key, part):
    picked = chosen_blocks(jax.random.fold_in(key, 11))
    return (picked % (D // 128)).astype(jnp.int32)


def draw_block_owner(key, part):
    keys = jax.random.split(jax.random.fold_in(key, 23), N_SECTION)

    def one_section(section_key):
        key_full, key_pop, key_noise, key_perm = jax.random.split(section_key, 4)
        slot_ids = jnp.arange(N_DP * CAP, dtype=jnp.int32)
        owner_of = slot_ids // CAP
        full_owner = jax.random.randint(key_full, (), 0, N_DP, dtype=jnp.int32)
        popular = jax.random.randint(key_pop, (N_DP,), 0, 4096, dtype=jnp.int32)
        noise = jax.random.randint(key_noise, (N_DP * CAP,), 0, 4096, dtype=jnp.int32)
        priority = noise + popular[owner_of] + jnp.where(owner_of == full_owner, 1 << 14, 0).astype(jnp.int32)
        scores = priority * 4096 + slot_ids
        _, taken = lax.top_k(scores, NB)
        owners = owner_of[taken]
        order = jax.random.permutation(key_perm, NB)
        return owners[order].astype(jnp.int32)
    return jax.vmap(one_section)(keys)


def level_of(stream_key, dims, shards, least, largest):
    def one(dim, blocks):
        heights = jax.random.uniform(jax.random.fold_in(jax.random.fold_in(stream_key, 6), dim), (blocks,), jnp.float32, least / len(shards), largest / len(shards))
        return jnp.repeat(jnp.exp(heights), dims[dim] // blocks).reshape((-1,) + (1,) * (len(dims) - dim - 1))

    level = one(*shards[0])
    for cut in shards[1:]:
        level = level * one(*cut)
    return level


def bell_draw(rng, dims, deviation, bound, cuts=(), held_as=jnp.bfloat16):
    entries = jax.random.normal(rng, dims, jnp.float32) * deviation
    if len(cuts) > 0:
        entries = level_of(rng, dims, cuts, -0.22, 0.18) * entries
    return jnp.clip(entries, min=-bound, max=bound).astype(held_as)


def setup_inputs(seed: int = 0) -> dict:
    seeds = jax.random.split(jax.random.key(seed), 10)
    d_out = bell_draw(seeds[0], (N_SECTION, TOKENS, D), 1.0, 6.0, ((0, 4), (1, 32)))
    down_weight = bell_draw(seeds[1], (N_SECTION, FF, D), FF ** -0.5, 0.0546875, ((0, 4), (1, 32)))
    gate_weight = bell_draw(seeds[2], (N_SECTION, FF, D), FF ** -0.5, 0.0546875, ((0, 4), (1, 32)))
    up_weight = bell_draw(seeds[3], (N_SECTION, FF, D), FF ** -0.5, 0.0546875, ((0, 4), (1, 32)))
    gate_pre = bell_draw(seeds[4], (N_SECTION, TOKENS, FF), 1.0, 6.0, ((0, 4), (1, 32)))
    up_val = bell_draw(seeds[5], (N_SECTION, TOKENS, FF), 1.0, 6.0, ((0, 4), (1, 32)))
    block_rows = draw_block_rows(jax.random.fold_in(seeds[9], 71), 0)
    block_cols = draw_block_cols(jax.random.fold_in(seeds[9], 71), 0)
    block_owner = draw_block_owner(jax.random.fold_in(seeds[9], 71), 0)
    return dict(d_out=d_out, down_weight=down_weight, gate_weight=gate_weight, up_weight=up_weight, gate_pre=gate_pre, up_val=up_val, block_rows=block_rows, block_cols=block_cols, block_owner=block_owner)


def gelu_pair(values):
    coeff = 0.7978845608
    cubic = values * values * values
    tangent = jnp.tanh(coeff * (values + 0.044715 * cubic))
    activated = 0.5 * values * (1.0 + tangent)
    slope = 0.5 * (1.0 + tangent) + 0.5 * values * (1.0 - tangent * tangent) * coeff * (1.0 + 3.0 * 0.044715 * values * values)
    return activated, slope


def owner_slots(owners):
    count_blocks = owners.shape[0]
    same = owners[:, None] == owners[None, :]
    index_list = jnp.arange(count_blocks, dtype=jnp.int32)
    earlier = index_list[None, :] < index_list[:, None]
    return jnp.sum((same & earlier).astype(jnp.int32), axis=1).astype(jnp.int32)


def reference(d_out, down_weight, gate_weight, up_weight, gate_pre, up_val, block_rows, block_cols, block_owner):
    inputs = []
    all_blocks = []
    group = FF // N_DP
    for section_id in range(N_SECTION):
        grad_rows = d_out[section_id]
        weight = down_weight[section_id]
        dhidden = lax.dot_general(grad_rows, weight, (((1,), (1,)), ((), ())), preferred_element_type=jnp.float32).astype(jnp.bfloat16)
        gate_val = gate_pre[section_id].astype(jnp.float32)
        up_vals = up_val[section_id].astype(jnp.float32)
        activated, slope = gelu_pair(gate_val)
        dh_wide = dhidden.astype(jnp.float32)
        local_gate = (dh_wide * up_vals * slope).astype(jnp.bfloat16)
        local_up = (dh_wide * activated).astype(jnp.bfloat16)
        w_gate = gate_weight[section_id]
        w_up = up_weight[section_id]

        def group_term(total, group_id):
            first = (group_id * group).astype(jnp.int32)
            g_part = lax.dynamic_slice_in_dim(local_gate, first, group, 1)
            u_part = lax.dynamic_slice_in_dim(local_up, first, group, 1)
            wg_part = lax.dynamic_slice_in_dim(w_gate, first, group, 0)
            wu_part = lax.dynamic_slice_in_dim(w_up, first, group, 0)
            term = jnp.dot(g_part, wg_part, preferred_element_type=jnp.float32) + jnp.dot(u_part, wu_part, preferred_element_type=jnp.float32)
            term = lax.optimization_barrier(term.astype(jnp.bfloat16))
            return total + term.astype(jnp.float32), None

        dx_total, _ = lax.scan(group_term, jnp.zeros((TOKENS, D), jnp.float32), jnp.arange(N_DP, dtype=jnp.int32))
        inputs.append(dx_total.astype(jnp.bfloat16))

        hidden = (activated * up_vals).astype(jnp.bfloat16)
        row_ids = block_rows[section_id]
        col_ids = block_cols[section_id]
        hidden_sel = jnp.take(hidden.reshape(TOKENS, FF // 128, 128), row_ids, axis=1)
        grad_sel = jnp.take(grad_rows.reshape(TOKENS, D // 128, 128), col_ids, axis=1)

        def replica(total, replica_id):
            first_row = (replica_id * TOK_DEV).astype(jnp.int32)
            h_part = lax.dynamic_slice_in_dim(hidden_sel, first_row, TOK_DEV, 0).astype(jnp.float32)
            g_part = lax.dynamic_slice_in_dim(grad_sel, first_row, TOK_DEV, 0).astype(jnp.float32)
            term = jnp.einsum("tnf,tnd->nfd", h_part, g_part).astype(jnp.bfloat16)
            term = lax.optimization_barrier(term)
            return total + term.astype(jnp.float32), None

        start_total = jnp.zeros((NB, 128, 128), jnp.float32)
        summed, _ = lax.scan(replica, start_total, jnp.arange(N_DP, dtype=jnp.int32))
        summed = summed * (1.0 / N_DP)
        owners = block_owner[section_id]
        positions = owners * CAP + owner_slots(owners)
        buffer = jnp.zeros((N_DP * CAP, 128, 128), jnp.float32).at[positions].set(summed)
        all_blocks.append(buffer.astype(jnp.bfloat16))
    zero_rows = jnp.zeros((TOKENS, D), jnp.bfloat16)
    grad_input = jnp.stack(inputs[1:] + [zero_rows])
    return grad_input, jnp.stack(all_blocks)
```

```python
import jax
import jax.numpy as jnp
from jax import lax
from jax.sharding import PartitionSpec as P

CAP = 3


def passed_along(value, axis, by):
    devices = lax.axis_size(axis)
    pairs = [(i, i + by) for i in range(devices) if 0 <= i + by < devices]
    return lax.ppermute(value, axis, pairs)


def gelu_pair(values):
    coeff = 0.7978845608
    cubic = values * values * values
    tangent = jnp.tanh(coeff * (values + 0.044715 * cubic))
    activated = 0.5 * values * (1.0 + tangent)
    slope = 0.5 * (1.0 + tangent) + 0.5 * values * (1.0 - tangent * tangent) * coeff * (
        1.0 + 3.0 * 0.044715 * values * values
    )
    return (activated, slope)


def owner_slots(owners):
    count_blocks = owners.shape[0]
    same = owners[:, None] == owners[None, :]
    index_list = jnp.arange(count_blocks, dtype=jnp.int32)
    earlier = index_list[None, :] < index_list[:, None]
    return jnp.sum((same & earlier).astype(jnp.int32), axis=1)


def shards(
    d_out,
    down_weight,
    gate_weight,
    up_weight,
    gate_pre,
    up_val,
    block_rows,
    block_cols,
    block_owner,
):
    grad_rows = d_out[0]
    w_shard = down_weight[0]
    w_gate = gate_weight[0]
    w_up = up_weight[0]
    tok_rows = grad_rows.shape[0]
    replicas = lax.axis_size("dp")
    row_ids = block_rows[0]
    col_ids = block_cols[0]
    owners = block_owner[0]
    count_blocks = row_ids.shape[0]
    position = owners * CAP + owner_slots(owners)
    slot_ids = jnp.arange(replicas * CAP, dtype=jnp.int32)
    match = position[None, :] == slot_ids[:, None]
    block_list = jnp.arange(count_blocks, dtype=jnp.int32)
    slot_rows = jnp.sum(jnp.where(match, row_ids[None, :], 0), axis=1)
    owner_index = lax.axis_index("dp")
    my_slots = owner_index * CAP + jnp.arange(CAP, dtype=jnp.int32)
    my_match = position[None, :] == my_slots[:, None]
    my_cols = jnp.sum(jnp.where(my_match, col_ids[None, :], 0), axis=1)
    present = jnp.any(my_match, axis=1)

    gate_local, up_local = gate_pre[0], up_val[0]
    gate_units = lax.all_to_all(gate_local, "dp", split_axis=1, concat_axis=0, tiled=True)
    up_units = lax.all_to_all(up_local, "dp", split_axis=1, concat_axis=0, tiled=True)
    every_row = lax.all_gather(grad_rows, "dp", axis=0, tiled=True)

    def in_slots(value):
        blocks = value.reshape(tok_rows, -1, 128)
        return jnp.take(blocks, slot_rows, axis=1).astype(jnp.float32)

    sel_gate, sel_up = in_slots(gate_local), in_slots(up_local)
    hidden_sel = (gelu_pair(sel_gate)[0] * sel_up).astype(jnp.bfloat16)
    hidden_mine = lax.all_to_all(hidden_sel, "dp", split_axis=1, concat_axis=0, tiled=True)

    dhidden = lax.dot_general(
        every_row, w_shard, (((1,), (1,)), ((), ())), preferred_element_type=jnp.float32
    ).astype(jnp.bfloat16)
    activated, slope = gelu_pair(gate_units.astype(jnp.float32))
    dh_wide = dhidden.astype(jnp.float32)
    local_gate = (dh_wide * up_units.astype(jnp.float32) * slope).astype(jnp.bfloat16)
    local_up = (dh_wide * activated).astype(jnp.bfloat16)
    summed_input = lax.psum_scatter(
        (
            jnp.dot(local_gate, w_gate, preferred_element_type=jnp.float32)
            + jnp.dot(local_up, w_up, preferred_element_type=jnp.float32)
        ).astype(jnp.bfloat16),
        "dp",
        scatter_dimension=0,
        tiled=True,
    )
    grad_input = passed_along(summed_input, "section", -1)
    grad_sel = jnp.take(every_row.reshape(every_row.shape[0], -1, 128), my_cols, axis=1)
    mine = jnp.einsum("tnf,tnd->nfd", hidden_mine, grad_sel, preferred_element_type=jnp.float32)
    mine = (mine * (1.0 / replicas)).astype(jnp.bfloat16)
    result = jnp.where(present[:, None, None], mine, jnp.zeros((), jnp.bfloat16))
    return (grad_input[None], result[None])


def solution(mesh):
    return jax.shard_map(
        shards,
        mesh=mesh,
        in_specs=(
            P("section", "dp", None),
            P("section", "dp", None),
            P("section", "dp", None),
            P("section", "dp", None),
            P("section", "dp", None),
            P("section", "dp", None),
            P("section", None),
            P("section", None),
            P("section", None),
        ),
        out_specs=(P("section", "dp", None), P("section", "dp", None, None)),
        check_vma=False,
    )
```

```python
import jax
import jax.numpy as jnp
from jax import lax
from jax.experimental import pallas as pl
from jax.experimental.pallas import tpu as pltpu
from jax.sharding import PartitionSpec as P

CAP = 3
MESH = pl.DeviceIdType.MESH
BF = jnp.bfloat16
F32 = jnp.float32
SIDE = 4
TOK = 48
WIDTH = 4096
UNITS = 352
WIN = 768
HALF = WIDTH // 2
QUART = WIDTH // 4


def gelu_pair(values):
    coeff = 0.7978845608
    cubic = values * values * values
    tangent = jnp.tanh(coeff * (values + 0.044715 * cubic))
    activated = 0.5 * values * (1.0 + tangent)
    slope = 0.5 * (1.0 + tangent) + 0.5 * values * (1.0 - tangent * tangent) * coeff * (
        1.0 + 3.0 * 0.044715 * values * values
    )
    return (activated, slope)


def owner_slots(owners):
    count_blocks = owners.shape[0]
    same = owners[:, None] == owners[None, :]
    index_list = jnp.arange(count_blocks, dtype=jnp.int32)
    earlier = index_list[None, :] < index_list[:, None]
    return jnp.sum((same & earlier).astype(jnp.int32), axis=1)


def kernel(
    slot_rows, slot_cols, d_out, w_down, w_gate, w_up, gate, up,
    grad_out, block_out,
    wd, wg, wu, x, gp, uq, lg, t, rb, rc, fin, gl, ul, xb, hs, hr, pb, pr,
    loc, w_send, w_recv, ag_send, ag_recv, a2_send, a2_recv, h_send, h_recv,
    rb_send, rb_recv, rc_send, rc_recv, x_send, x_recv, p_send, p_recv,
):
    sec = lax.axis_index("section")
    me = lax.axis_index("dp")
    core = lax.rem(me, 2)
    chip = lax.div(me, 2)
    yy = lax.div(chip, SIDE)
    zz = lax.rem(chip, SIDE)

    def dev(y, z):
        return (sec, (y * SIDE + z) * 2 + core)

    def step(p, by):
        return lax.rem(p + (by + SIDE), SIDE)

    partner = (sec, chip * 2 + (1 - core))
    prev_sec = (lax.rem(sec + 3, 4), me)
    next_sec = (lax.rem(sec + 1, 4), me)
    others = [(i, j) for i in range(SIDE) for j in range(SIDE) if (i, j) != (0, 0)]

    barrier = pltpu.get_barrier_semaphore()
    for dy, dz in others:
        pl.semaphore_signal(barrier, inc=1, device_id=dev(step(yy, dy), step(zz, dz)), device_id_type=MESH)
    for target in (partner, prev_sec, next_sec):
        pl.semaphore_signal(barrier, inc=1, device_id=target, device_id_type=MESH)

    started = []

    def send(src, dst, s_sem, r_sem, target):
        copy = pltpu.make_async_remote_copy(
            src_ref=src, dst_ref=dst, send_sem=s_sem, recv_sem=r_sem,
            device_id=target, device_id_type=MESH,
        )
        copy.start()
        started.append(copy)
        return copy

    pad = 64 * lax.rem(chip, 2)
    place = pl.multiple_of(pad + core * UNITS, 32)
    rows = pl.ds(place, UNITS)
    local = [
        pltpu.make_async_copy(d_out, x.at[yy, zz], loc.at[0]),
        pltpu.make_async_copy(w_down, wd.at[rows], loc.at[3]),
        pltpu.make_async_copy(w_gate, wg.at[rows], loc.at[4]),
        pltpu.make_async_copy(w_up, wu.at[rows], loc.at[5]),
    ]
    for copy in local:
        copy.start()

    def lanes_of(k):
        return pl.ds(pl.multiple_of(k * 128, 128), 128)

    def load_block(k, carry):
        pltpu.make_async_copy(gate.at[:, lanes_of(k)], gl.at[k], loc.at[1]).start()
        pltpu.make_async_copy(up.at[:, lanes_of(k)], ul.at[k], loc.at[2]).start()
        return carry

    lax.fori_loop(0, gl.shape[0], load_block, 0)
    pl.semaphore_wait(barrier, len(others) + 3)

    def along(half, first, by, p, q):
        if (half == 0) == first:
            return dev(step(yy, by), zz)
        return dev(yy, step(zz, by))

    pos = [(yy, zz), (zz, yy)]

    def at(half, p, q):
        return (p, q) if half == 0 else (q, p)

    def cols(half, part=None):
        if part is None:
            return pl.ds(half * HALF, HALF)
        return pl.ds(half * HALF + part * QUART, QUART)

    def piece(half, p, q, part=None):
        a, b = at(half, p, q)
        return x.at[a, b, :, cols(half, part)]

    def ag(half, k, src, dst, target):
        return send(src, dst, ag_send.at[half, k], ag_recv.at[half, k], target)

    got = {}
    near = (0, -1, 1, 2)

    def spread(half, j, from_input=False):
        p, q = pos[half]
        pj = step(p, near[j])
        src = d_out.at[:, cols(half)] if from_input else piece(half, pj, q)
        dst = piece(half, pj, q)
        for n, by in ((0, 1), (1, -1)):
            got[half, 4 + 4 * j + n] = ag(half, 4 + 4 * j + n, src, dst, along(half, False, by, p, q))

    def pass_on(half, j):
        p, q = pos[half]
        pj = step(p, near[j])
        for n, by in ((0, 1), (1, -1)):
            got[half, 4 + 4 * j + n].wait_recv()
            ref = piece(half, pj, step(q, -by), n)
            got[half, 6 + 4 * j + n] = ag(half, 6 + 4 * j + n, ref, ref, along(half, False, by, p, q))

    for half in (0, 1):
        p, q = pos[half]
        for n, by in ((0, 1), (1, -1)):
            got[half, n] = ag(half, n, d_out.at[:, cols(half)], piece(half, p, q), along(half, True, by, p, q))
    w_copies = []
    for n, (src, dst) in enumerate(((w_down, wd), (w_gate, wg), (w_up, wu))):
        w_copies.append(send(src, dst.at[rows], w_send.at[n], w_recv.at[n], partner))
    for half in (0, 1):
        spread(half, 0, True)
    zero_rows = pl.ds(pl.multiple_of(704 - 11 * pad, 64), 64)
    for ref in (wd, wg, wu):
        ref[zero_rows, :] = jnp.zeros((64, WIDTH), BF)

    for n, by in ((0, 1), (1, -1)):
        for half in (0, 1):
            p, q = pos[half]
            got[half, n].wait_recv()
            ref = piece(half, step(p, -by), q, n)
            got[half, 2 + n] = ag(half, 2 + n, ref, ref, along(half, True, by, p, q))
        for half in (0, 1):
            spread(half, 1 + n)
    for half in (0, 1):
        pass_on(half, 0)

    pltpu.make_async_copy(gl, gl, loc.at[1]).wait()
    pltpu.make_async_copy(ul, ul, loc.at[2]).wait()

    def one_slot(s, carry):
        g = gl[slot_rows[s]].astype(F32)
        u = ul[slot_rows[s]].astype(F32)
        hs[lax.div(s, 6), lax.rem(s, 6)] = (gelu_pair(g)[0] * u).astype(BF)
        return carry

    lax.fori_loop(0, 48, one_slot, 0)
    for half in (0, 1):
        got[half, 2].wait_recv()
        got[half, 3].wait_recv()
        spread(half, 3)

    def window(g):
        return pl.ds(pl.multiple_of(lax.div(g * 11, 2) * 128, 128), WIN)

    a2 = []
    for k, (dy, dz) in enumerate(others):
        ty, tz = step(yy, dy), step(zz, dz)
        win = window(ty * SIDE + tz)
        for n, (src, dst) in enumerate(((gate, gp), (up, uq))):
            a2.append(send(src.at[:, win], dst.at[yy, zz], a2_send.at[n, k], a2_recv.at[n, k], dev(ty, tz)))
    mine = window(chip)
    own = [
        pltpu.make_async_copy(gate.at[:, mine], gp.at[yy, zz], loc.at[6]),
        pltpu.make_async_copy(up.at[:, mine], uq.at[yy, zz], loc.at[7]),
    ]
    for copy in own:
        copy.start()
    for half in (0, 1):
        pass_on(half, 1)
        pass_on(half, 2)
    lax.fori_loop(48, 96, one_slot, 0)
    for half in (0, 1):
        pass_on(half, 3)
    for j in range(4):
        for half in (0, 1):
            got[half, 6 + 4 * j].wait_recv()
            got[half, 7 + 4 * j].wait_recv()

    hid = []
    for k, (dy, dz) in enumerate(others):
        ty, tz = step(yy, dy), step(zz, dz)
        hid.append(send(hs.at[ty * SIDE + tz], hr.at[chip], h_send.at[k], h_recv.at[k], dev(ty, tz)))
    own_h = pltpu.make_async_copy(hs.at[chip], hr.at[chip], loc.at[8])
    own_h.start()

    local[0].wait()

    def copy_block(k, carry):
        pltpu.make_async_copy(x.at[:, :, :, lanes_of(k)], xb.at[k], loc.at[9]).start()
        return carry

    lax.fori_loop(0, xb.shape[0], copy_block, 0)
    local[1].wait()
    w_copies[0].wait_recv()

    def dh_tile(i, carry):
        n = lax.div(i, 2)
        m = lax.rem(i, 2)
        units = pl.ds(pl.multiple_of(n * 256, 256), 256)
        a = x[pl.ds(m * 2, 2)].reshape(2 * SIDE * TOK, WIDTH)
        out = lax.dot_general(a, wd[units, :], (((1,), (1,)), ((), ())), preferred_element_type=F32)
        lg[pl.ds(m * 2, 2), :, :, units] = out.astype(BF).reshape(2, SIDE, TOK, 256)
        return carry

    lax.fori_loop(0, 6, dh_tile, 0)

    for copy in own:
        copy.wait()
    for copy in a2:
        copy.wait_recv()

    def point(i, carry):
        a, b = lax.div(i, SIDE), lax.rem(i, SIDE)
        for k in range(WIN // 128):
            lane = pl.ds(k * 128, 128)
            activated, slope = gelu_pair(gp[a, b, :, lane].astype(F32))
            dh = lg[a, b, :, lane].astype(F32)
            u = uq[a, b, :, lane].astype(F32)
            lg[a, b, :, lane] = (dh * u * slope).astype(BF)
            gp[a, b, :, lane] = (dh * activated).astype(BF)
        return carry

    lax.fori_loop(0, SIDE * SIDE, point, 0)
    for n in (2, 3):
        local[n].wait()
    for n in (1, 2):
        w_copies[n].wait_recv()

    def group(half, ref, p, lanes):
        if half == 0:
            return ref[p, :, :, lanes]
        return ref[:, p, :, lanes]

    def put(half, ref, p, lanes, value):
        if half == 0:
            ref[p, :, :, lanes] = value
        else:
            ref[:, p, :, lanes] = value

    def view(half, ref, p, lanes):
        if half == 0:
            return ref.at[p, :, :, lanes]
        return ref.at[:, p, :, lanes]

    def terms(half, targets):
        def tile(i, carry):
            lanes = pl.ds(pl.multiple_of(half * HALF + i * 256, 256), 256)
            every = pl.ds(0, WIN)
            ga = jnp.concatenate([group(half, lg, p, every).reshape(SIDE * TOK, WIN) for p in targets], axis=0)
            ua = jnp.concatenate([group(half, gp, p, every).reshape(SIDE * TOK, WIN) for p in targets], axis=0)
            out = jnp.dot(ga, wg[:, lanes], preferred_element_type=F32)
            out = out + jnp.dot(ua, wu[:, lanes], preferred_element_type=F32)
            out = out.astype(BF)
            for k, p in enumerate(targets):
                part = out[k * SIDE * TOK : (k + 1) * SIDE * TOK]
                put(half, t, p, lanes, part.reshape(SIDE, TOK, 256))
            return carry

        lax.fori_loop(0, HALF // 256, tile, 0)

    r1 = {}

    def rs1(half, k, p_of, part, by):
        p, q = pos[half]
        r1[half, k] = send(
            view(half, t, p_of, cols(half, part)), rb.at[half, k],
            rb_send.at[half, k], rb_recv.at[half, k], along(half, True, by, p, q),
        )

    for half in (0, 1):
        p, q = pos[half]
        terms(half, [step(p, 2)])
        rs1(half, 0, step(p, 2), 0, 1)
        rs1(half, 1, step(p, 2), 1, -1)
    for half in (0, 1):
        p, q = pos[half]
        terms(half, [step(p, 1), step(p, -1)])
        rs1(half, 2, step(p, 1), 1, 1)
        rs1(half, 3, step(p, -1), 0, -1)

    def add_rows(half, dst_p, part, bufs):
        lanes = cols(half, part)

        def row(i, carry):
            if half == 0:
                total = t[dst_p, i, :, lanes].astype(F32)
            else:
                total = t[i, dst_p, :, lanes].astype(F32)
            for k in bufs:
                total = total + rb[half, k, i].astype(F32)
            if half == 0:
                t[dst_p, i, :, lanes] = total.astype(BF)
            else:
                t[i, dst_p, :, lanes] = total.astype(BF)
            return carry

        lax.fori_loop(0, SIDE, row, 0)

    for half in (0, 1):
        p, q = pos[half]
        r1[half, 0].wait_recv()
        add_rows(half, step(p, 1), 0, (0,))
        rs1(half, 4, step(p, 1), 0, 1)
        r1[half, 1].wait_recv()
        add_rows(half, step(p, -1), 1, (1,))
        rs1(half, 5, step(p, -1), 1, -1)
    for half in (0, 1):
        terms(half, [pos[half][0]])

    own_h.wait()
    for copy in hid:
        copy.wait_recv()
    pltpu.make_async_copy(xb, xb, loc.at[9]).wait()
    for s in range(6):
        h = hr[:, s].reshape(SIDE * SIDE * TOK, 128)
        d = xb[slot_cols[s]].reshape(SIDE * SIDE * TOK, 128)
        pb[s] = lax.dot_general(h, d, (((0,), (0,)), ((), ())), preferred_element_type=F32)
    p_copy = send(pb.at[pl.ds((1 - core) * CAP, CAP)], pr, p_send.at[0], p_recv.at[0], partner)

    r2 = {}

    def piece_t(half, q_of, part):
        a, b = at(half, pos[half][0], q_of)
        return (a, b, slice(None), cols(half, part))

    def rs2(half, k, q_of, part, by):
        p, q = pos[half]
        r2[half, k] = send(
            t.at[piece_t(half, q_of, part)], rc.at[half, k],
            rc_send.at[half, k], rc_recv.at[half, k], along(half, False, by, p, q),
        )

    for half in (0, 1):
        p, q = pos[half]
        for k in (2, 3, 4, 5):
            r1[half, k].wait_recv()
        add_rows(half, p, 0, (3, 4))
        add_rows(half, p, 1, (2, 5))
        rs2(half, 0, step(q, 2), 0, 1)
        rs2(half, 1, step(q, 2), 1, -1)
        rs2(half, 2, step(q, 1), 1, 1)
        rs2(half, 3, step(q, -1), 0, -1)
    for half in (0, 1):
        p, q = pos[half]
        for k, by in ((0, 1), (1, -1)):
            r2[half, k].wait_recv()
            here = piece_t(half, step(q, by), k)
            t[here] = (t[here].astype(F32) + rc[half, k].astype(F32)).astype(BF)
            rs2(half, 4 + k, step(q, by), k, by)
    last = []
    for half in (0, 1):
        p, q = pos[half]
        for k in (2, 3, 4, 5):
            r2[half, k].wait_recv()
        for part, bufs in ((0, (3, 4)), (1, (2, 5))):
            total = t[piece_t(half, q, part)].astype(F32)
            for k in bufs:
                total = total + rc[half, k].astype(F32)
            fin[:, cols(half, part)] = total.astype(BF)
        last.append(send(
            fin.at[:, cols(half)], grad_out.at[:, cols(half)],
            x_send.at[half], x_recv.at[half], prev_sec,
        ))
    p_copy.wait_recv()
    block_out[...] = ((pb[pl.ds(core * CAP, CAP)] + pr[...]) * (1.0 / 32.0)).astype(BF)
    for copy in last:
        copy.wait_recv()
    for copy in started:
        copy.wait_send()


def shards(d_out, down_weight, gate_weight, up_weight, gate_pre, up_val, block_rows, block_cols, block_owner):
    row_ids, col_ids, owners = block_rows[0], block_cols[0], block_owner[0]
    replicas = lax.axis_size("dp")
    position = owners * CAP + owner_slots(owners)
    slot_ids = jnp.arange(replicas * CAP, dtype=jnp.int32)
    match = position[None, :] == slot_ids[:, None]
    slot_rows = jnp.sum(jnp.where(match, row_ids[None, :], 0), axis=1)
    me = lax.axis_index("dp")
    chip_slots = (me // 2) * (2 * CAP) + jnp.arange(2 * CAP, dtype=jnp.int32)
    slot_cols = jnp.sum(jnp.where(position[None, :] == chip_slots[:, None], col_ids[None, :], 0), axis=1)
    my_slots = me * CAP + jnp.arange(CAP, dtype=jnp.int32)
    present = jnp.any(position[None, :] == my_slots[:, None], axis=1)

    smem = pl.BlockSpec(memory_space=pltpu.SMEM)
    hbm = pl.BlockSpec(memory_space=pl.ANY)
    dma = pltpu.SemaphoreType.DMA
    grid_shape = (SIDE, SIDE, TOK)
    grad, blocks = pl.pallas_call(
        kernel,
        out_shape=(
            jax.ShapeDtypeStruct((TOK, WIDTH), BF),
            jax.ShapeDtypeStruct((CAP, 128, 128), BF),
        ),
        in_specs=[smem, smem] + [hbm] * 6,
        out_specs=(hbm, pl.BlockSpec(memory_space=pltpu.VMEM)),
        scratch_shapes=[
            pltpu.VMEM((WIN, WIDTH), BF),
            pltpu.VMEM((WIN, WIDTH), BF),
            pltpu.VMEM((WIN, WIDTH), BF),
            pltpu.VMEM((*grid_shape, WIDTH), BF),
            pltpu.VMEM((*grid_shape, WIN), BF),
            pltpu.VMEM((*grid_shape, WIN), BF),
            pltpu.VMEM((*grid_shape, WIN), BF),
            pltpu.VMEM((*grid_shape, WIDTH), BF),
            pltpu.VMEM((2, 6, SIDE, TOK, QUART), BF),
            pltpu.VMEM((2, 6, TOK, QUART), BF),
            pltpu.VMEM((TOK, WIDTH), BF),
            pltpu.VMEM((88, TOK, 128), BF),
            pltpu.VMEM((88, TOK, 128), BF),
            pltpu.VMEM((32, *grid_shape, 128), BF),
            pltpu.VMEM((16, 6, TOK, 128), BF),
            pltpu.VMEM((16, 6, TOK, 128), BF),
            pltpu.VMEM((6, 128, 128), F32),
            pltpu.VMEM((CAP, 128, 128), F32),
            dma((10,)),
            dma((3,)), dma((3,)),
            dma((2, 20)), dma((2, 20)),
            dma((2, 15)), dma((2, 15)),
            dma((15,)), dma((15,)),
            dma((2, 6)), dma((2, 6)),
            dma((2, 6)), dma((2, 6)),
            dma((2,)), dma((2,)),
            dma((1,)), dma((1,)),
        ],
        compiler_params=pltpu.CompilerParams(
            collective_id=0, has_side_effects=True, vmem_limit_bytes=62 * 1024 * 1024
        ),
        name="relay",
    )(slot_rows, slot_cols, d_out[0], down_weight[0], gate_weight[0], up_weight[0], gate_pre[0], up_val[0])
    last = lax.axis_index("section") == lax.axis_size("section") - 1
    grad = jnp.where(last, jnp.zeros((), BF), grad)
    result = jnp.where(present[:, None, None], blocks, jnp.zeros((), BF))
    return (grad[None], result[None])


def solution(mesh):
    return jax.shard_map(
        shards,
        mesh=mesh,
        in_specs=(P("section", "dp", None),) * 6 + (P("section", None),) * 3,
        out_specs=(P("section", "dp", None), P("section", "dp", None, None)),
        check_vma=False,
    )
```

```python
import jax
import jax.numpy as jnp
from jax import lax
from jax.experimental import pallas as pl
from jax.experimental.pallas import tpu as pltpu
from jax.sharding import PartitionSpec as P

CAP = 3
MESH = pl.DeviceIdType.MESH
BF = jnp.bfloat16
F32 = jnp.float32
SIDE = 4
TOK = 48
WIDTH = 4096
UNITS = 352
WIN = 768
HALF = WIDTH // 2
QUART = WIDTH // 4
CHUNKS = ((0, 1280), (1280, 768))


def gelu_pair(values):
    coeff = 0.7978845608
    cubic = values * values * values
    tangent = jnp.tanh(coeff * (values + 0.044715 * cubic))
    activated = 0.5 * values * (1.0 + tangent)
    slope = 0.5 * (1.0 + tangent) + 0.5 * values * (1.0 - tangent * tangent) * coeff * (
        1.0 + 3.0 * 0.044715 * values * values
    )
    return (activated, slope)


def kernel(
    block_rows, block_cols, block_owner, d_out, w_down, w_gate, w_up, gate, up,
    grad_out, block_out,
    wd, wg, wu, x, gp, uq, lg, t, rb, rc, fin, gl, ul, xb, hs, hr, pb, pr, tab, slots,
    loc, w_send, w_recv, ag_send, ag_recv, a2_send, a2_recv, h_send, h_recv,
    rb_send, rb_recv, rc_send, rc_recv, x_send, x_recv, p_send, p_recv,
):
    sec = lax.axis_index("section")
    me = lax.axis_index("dp")
    core = lax.rem(me, 2)
    chip = lax.div(me, 2)
    yy = lax.div(chip, SIDE)
    zz = lax.rem(chip, SIDE)

    def dev(y, z):
        return (sec, (y * SIDE + z) * 2 + core)

    def step(p, by):
        return lax.rem(p + (by + SIDE), SIDE)

    partner = (sec, chip * 2 + (1 - core))
    prev_sec = (lax.rem(sec + 3, 4), me)
    next_sec = (lax.rem(sec + 1, 4), me)
    others = [(i, j) for i in range(SIDE) for j in range(SIDE) if (i, j) != (0, 0)]
    others.sort(key=lambda d: -(min(d[0], SIDE - d[0]) + min(d[1], SIDE - d[1])))

    barrier = pltpu.get_barrier_semaphore()
    for dy, dz in others:
        pl.semaphore_signal(barrier, inc=1, device_id=dev(step(yy, dy), step(zz, dz)), device_id_type=MESH)
    for target in (partner, prev_sec, next_sec):
        pl.semaphore_signal(barrier, inc=1, device_id=target, device_id_type=MESH)

    started = []

    def send(src, dst, s_sem, r_sem, target):
        copy = pltpu.make_async_remote_copy(
            src_ref=src, dst_ref=dst, send_sem=s_sem, recv_sem=r_sem,
            device_id=target, device_id_type=MESH,
        )
        copy.start()
        started.append(copy)
        return copy

    pad = 64 * lax.rem(chip, 2)
    place = pl.multiple_of(pad + core * UNITS, 32)
    rows = pl.ds(place, UNITS)
    local = [
        pltpu.make_async_copy(d_out, x.at[yy, zz], loc.at[0]),
        pltpu.make_async_copy(w_down, wd.at[rows], loc.at[3]),
        pltpu.make_async_copy(w_gate, wg.at[rows], loc.at[4]),
        pltpu.make_async_copy(w_up, wu.at[rows], loc.at[5]),
    ]
    for copy in local:
        copy.start()

    def lanes_of(k):
        return pl.ds(pl.multiple_of(k * 128, 128), 128)

    def load_block(k, carry):
        pltpu.make_async_copy(gate.at[:, lanes_of(k)], gl.at[k], loc.at[1]).start()
        pltpu.make_async_copy(up.at[:, lanes_of(k)], ul.at[k], loc.at[2]).start()
        return carry

    lax.fori_loop(0, gl.shape[0], load_block, 0)
    pl.semaphore_wait(barrier, len(others) + 3)

    def along(half, first, by, p, q):
        if (half == 0) == first:
            return dev(step(yy, by), zz)
        return dev(yy, step(zz, by))

    pos = [(yy, zz), (zz, yy)]

    def at(half, p, q):
        return (p, q) if half == 0 else (q, p)

    def cols(half, part=None):
        if part is None:
            return pl.ds(half * HALF, HALF)
        return pl.ds(half * HALF + part * QUART, QUART)

    def piece(half, p, q, part=None):
        a, b = at(half, p, q)
        return x.at[a, b, :, cols(half, part)]

    def ag(half, k, src, dst, target):
        return send(src, dst, ag_send.at[half, k], ag_recv.at[half, k], target)

    got = {}
    near = (0, -1, 1, 2)

    def spread(half, j, from_input=False):
        p, q = pos[half]
        pj = step(p, near[j])
        src = d_out.at[:, cols(half)] if from_input else piece(half, pj, q)
        dst = piece(half, pj, q)
        for n, by in ((0, 1), (1, -1)):
            got[half, 4 + 4 * j + n] = ag(half, 4 + 4 * j + n, src, dst, along(half, False, by, p, q))

    def pass_on(half, j):
        p, q = pos[half]
        pj = step(p, near[j])
        for n, by in ((0, 1), (1, -1)):
            got[half, 4 + 4 * j + n].wait_recv()
            ref = piece(half, pj, step(q, -by), n)
            got[half, 6 + 4 * j + n] = ag(half, 6 + 4 * j + n, ref, ref, along(half, False, by, p, q))

    for half in (0, 1):
        p, q = pos[half]
        for n, by in ((0, 1), (1, -1)):
            got[half, n] = ag(half, n, d_out.at[:, cols(half)], piece(half, p, q), along(half, True, by, p, q))
    w_copies = []
    for n, (src, dst) in enumerate(((w_down, wd), (w_gate, wg), (w_up, wu))):
        w_copies.append(send(src, dst.at[rows], w_send.at[n], w_recv.at[n], partner))
    for half in (0, 1):
        spread(half, 0, True)
    zero_rows = pl.ds(pl.multiple_of(704 - 11 * pad, 64), 64)
    for ref in (wd, wg, wu):
        ref[zero_rows, :] = jnp.zeros((64, WIDTH), BF)

    for n, by in ((0, 1), (1, -1)):
        for half in (0, 1):
            p, q = pos[half]
            got[half, n].wait_recv()
            ref = piece(half, step(p, -by), q, n)
            got[half, 2 + n] = ag(half, 2 + n, ref, ref, along(half, True, by, p, q))
        for half in (0, 1):
            spread(half, 1 + n)
    for half in (0, 1):
        pass_on(half, 0)

    blocks = block_owner.shape[1]
    row_id = lax.broadcasted_iota(jnp.int32, (blocks, blocks), 0)
    col_id = lax.broadcasted_iota(jnp.int32, (blocks, blocks), 1)

    def upright(ref):
        wide = jnp.broadcast_to(ref[...], (blocks, blocks))
        return jnp.sum(jnp.where(row_id == col_id, wide, 0), axis=1, keepdims=True)

    owner = upright(block_owner)
    earlier = (block_owner[...] == owner) & (col_id < row_id)
    position = owner * CAP + jnp.sum(jnp.where(earlier, 1, 0), axis=1, keepdims=True)
    match = position == lax.broadcasted_iota(jnp.int32, (blocks, 128), 1)
    for k, value in enumerate((upright(block_rows), upright(block_cols), jnp.ones((blocks, 1), jnp.int32))):
        tab[k : k + 1, :] = jnp.sum(jnp.where(match, value, 0), axis=0, keepdims=True)
    tables = pltpu.make_async_copy(tab, slots, loc.at[10])
    tables.start()
    tables.wait()

    pltpu.make_async_copy(gl, gl, loc.at[1]).wait()
    pltpu.make_async_copy(ul, ul, loc.at[2]).wait()

    def one_slot(s, carry):
        g = gl[slots[0, s]].astype(F32)
        u = ul[slots[0, s]].astype(F32)
        hs[lax.div(s, 6), lax.rem(s, 6)] = (gelu_pair(g)[0] * u).astype(BF)
        return carry

    lax.fori_loop(0, 48, one_slot, 0)
    for half in (0, 1):
        got[half, 2].wait_recv()
        got[half, 3].wait_recv()
        spread(half, 3)

    def window(g):
        return pl.ds(pl.multiple_of(lax.div(g * 11, 2) * 128, 128), WIN)

    a2 = []
    for n, (src, dst) in enumerate(((gate, gp), (up, uq))):
        for k, (dy, dz) in enumerate(others):
            ty, tz = step(yy, dy), step(zz, dz)
            win = window(ty * SIDE + tz)
            a2.append(send(src.at[:, win], dst.at[yy, zz], a2_send.at[n, k], a2_recv.at[n, k], dev(ty, tz)))
    mine = window(chip)
    own = [
        pltpu.make_async_copy(gate.at[:, mine], gp.at[yy, zz], loc.at[6]),
        pltpu.make_async_copy(up.at[:, mine], uq.at[yy, zz], loc.at[7]),
    ]
    for copy in own:
        copy.start()
    for half in (0, 1):
        pass_on(half, 1)
        pass_on(half, 2)
    lax.fori_loop(48, 96, one_slot, 0)
    for half in (0, 1):
        pass_on(half, 3)
    for j in range(4):
        for half in (0, 1):
            got[half, 6 + 4 * j].wait_recv()
            got[half, 7 + 4 * j].wait_recv()

    hid = []
    for k, (dy, dz) in enumerate(others):
        ty, tz = step(yy, dy), step(zz, dz)
        hid.append(send(hs.at[ty * SIDE + tz], hr.at[chip], h_send.at[k], h_recv.at[k], dev(ty, tz)))
    own_h = pltpu.make_async_copy(hs.at[chip], hr.at[chip], loc.at[8])
    own_h.start()

    local[0].wait()

    def copy_block(k, carry):
        pltpu.make_async_copy(x.at[:, :, :, lanes_of(k)], xb.at[k], loc.at[9]).start()
        return carry

    lax.fori_loop(0, xb.shape[0], copy_block, 0)
    local[1].wait()
    w_copies[0].wait_recv()

    def dh_tile(i, carry):
        n = lax.div(i, 2)
        m = lax.rem(i, 2)
        units = pl.ds(pl.multiple_of(n * 256, 256), 256)
        a = x[pl.ds(m * 2, 2)].reshape(2 * SIDE * TOK, WIDTH)
        out = lax.dot_general(a, wd[units, :], (((1,), (1,)), ((), ())), preferred_element_type=F32)
        lg[pl.ds(m * 2, 2), :, :, units] = out.astype(BF).reshape(2, SIDE, TOK, 256)
        return carry

    lax.fori_loop(0, 6, dh_tile, 0)

    for copy in own:
        copy.wait()
    for copy in a2:
        copy.wait_recv()

    def point(i, carry):
        a, b = lax.div(i, SIDE), lax.rem(i, SIDE)
        for k in range(WIN // 128):
            lane = pl.ds(k * 128, 128)
            activated, slope = gelu_pair(gp[a, b, :, lane].astype(F32))
            dh = lg[a, b, :, lane].astype(F32)
            u = uq[a, b, :, lane].astype(F32)
            lg[a, b, :, lane] = (dh * u * slope).astype(BF)
            gp[a, b, :, lane] = (dh * activated).astype(BF)
        return carry

    lax.fori_loop(0, SIDE * SIDE, point, 0)
    for n in (2, 3):
        local[n].wait()
    for n in (1, 2):
        w_copies[n].wait_recv()

    def group(half, ref, p, lanes):
        if half == 0:
            return ref[p, :, :, lanes]
        return ref[:, p, :, lanes]

    def put(half, ref, p, lanes, value):
        if half == 0:
            ref[p, :, :, lanes] = value
        else:
            ref[:, p, :, lanes] = value

    def view(half, ref, p, lanes):
        if half == 0:
            return ref.at[p, :, :, lanes]
        return ref.at[:, p, :, lanes]

    def terms(half, c, targets):
        first, width = CHUNKS[c]

        def tile(i, carry):
            lanes = pl.ds(pl.multiple_of(half * HALF + first + i * 256, 256), 256)
            every = pl.ds(0, WIN)
            ga = jnp.concatenate([group(half, lg, p, every).reshape(SIDE * TOK, WIN) for p in targets], axis=0)
            ua = jnp.concatenate([group(half, gp, p, every).reshape(SIDE * TOK, WIN) for p in targets], axis=0)
            out = jnp.dot(ga, wg[:, lanes], preferred_element_type=F32)
            out = out + jnp.dot(ua, wu[:, lanes], preferred_element_type=F32)
            out = out.astype(BF)
            for k, p in enumerate(targets):
                part = out[k * SIDE * TOK : (k + 1) * SIDE * TOK]
                put(half, t, p, lanes, part.reshape(SIDE, TOK, 256))
            return carry

        lax.fori_loop(0, width // 256, tile, 0)

    def lanes_at(half, c, part):
        first, width = CHUNKS[c]
        return pl.ds(half * HALF + first + part * (width // 2), width // 2)

    def held(c):
        first, width = CHUNKS[c]
        return pl.ds(first // 2, width // 2)

    r1, r2 = {}, {}

    def rs1(half, c, k, by, part):
        p, q = pos[half]
        p_of = step(p, 2) if k < 2 else step(p, by)
        r1[half, c, k] = send(
            view(half, t, p_of, lanes_at(half, c, part)), rb.at[half, k, :, :, held(c)],
            rb_send.at[half, 6 * c + k], rb_recv.at[half, 6 * c + k], along(half, True, by, p, q),
        )

    def add_rows(half, c, dst_p, part, bufs):
        lanes = lanes_at(half, c, part)

        def row(i, carry):
            if half == 0:
                total = t[dst_p, i, :, lanes].astype(F32)
            else:
                total = t[i, dst_p, :, lanes].astype(F32)
            for k in bufs:
                total = total + rb[half, k, i, :, held(c)].astype(F32)
            if half == 0:
                t[dst_p, i, :, lanes] = total.astype(BF)
            else:
                t[i, dst_p, :, lanes] = total.astype(BF)
            return carry

        lax.fori_loop(0, SIDE, row, 0)

    def far(c):
        for half in (0, 1):
            terms(half, c, [step(pos[half][0], 2)])
            rs1(half, c, 0, 1, 0)
            rs1(half, c, 1, -1, 1)

    def near_terms(c):
        for half in (0, 1):
            p, q = pos[half]
            terms(half, c, [step(p, 1), step(p, -1)])
            rs1(half, c, 2, 1, 1)
            rs1(half, c, 3, -1, 0)

    def own_terms(c):
        for half in (0, 1):
            terms(half, c, [pos[half][0]])

    def relay(c):
        for k, by in ((0, 1), (1, -1)):
            for half in (0, 1):
                r1[half, c, k].wait_recv()
                add_rows(half, c, step(pos[half][0], by), k, (k,))
                rs1(half, c, 4 + k, by, k)

    def piece_t(half, c, q_of, part):
        a, b = at(half, pos[half][0], q_of)
        return (a, b, slice(None), lanes_at(half, c, part))

    def rs2(half, c, k, q_of, part, by):
        p, q = pos[half]
        r2[half, c, k] = send(
            t.at[piece_t(half, c, q_of, part)], rc.at[half, k, :, held(c)],
            rc_send.at[half, 6 * c + k], rc_recv.at[half, 6 * c + k], along(half, False, by, p, q),
        )

    def turn(c):
        for half in (0, 1):
            p, q = pos[half]
            for k in (2, 3, 4, 5):
                r1[half, c, k].wait_recv()
            add_rows(half, c, p, 0, (3, 4))
            add_rows(half, c, p, 1, (2, 5))
            rs2(half, c, 0, step(q, 2), 0, 1)
            rs2(half, c, 1, step(q, 2), 1, -1)
            rs2(half, c, 2, step(q, 1), 1, 1)
            rs2(half, c, 3, step(q, -1), 0, -1)

    def relay2(c):
        for k, by in ((0, 1), (1, -1)):
            for half in (0, 1):
                q = pos[half][1]
                r2[half, c, k].wait_recv()
                here = piece_t(half, c, step(q, by), k)
                t[here] = (t[here].astype(F32) + rc[half, k, :, held(c)].astype(F32)).astype(BF)
                rs2(half, c, 4 + k, step(q, by), k, by)

    kept = jnp.minimum(sec, 1).astype(F32)
    last = []

    def finish(c):
        first, width = CHUNKS[c]
        for half in (0, 1):
            p, q = pos[half]
            for k in (2, 3, 4, 5):
                r2[half, c, k].wait_recv()
            for part, bufs in ((0, (3, 4)), (1, (2, 5))):
                total = t[piece_t(half, c, q, part)].astype(F32)
                for k in bufs:
                    total = total + rc[half, k, :, held(c)].astype(F32)
                fin[:, lanes_at(half, c, part)] = (total * kept).astype(BF)
            lanes = pl.ds(half * HALF + first, width)
            last.append(send(
                fin.at[:, lanes], grad_out.at[:, lanes],
                x_send.at[half, c], x_recv.at[half, c], prev_sec,
            ))

    far(0)
    near_terms(0)
    far(1)
    relay(0)
    own_terms(0)
    near_terms(1)
    own_terms(1)
    turn(0)
    relay(1)
    relay2(0)

    own_h.wait()
    for copy in hid:
        copy.wait_recv()
    pltpu.make_async_copy(xb, xb, loc.at[9]).wait()
    for s in range(6):
        h = hr[:, s].reshape(SIDE * SIDE * TOK, 128)
        d = xb[slots[1, chip * 6 + s]].reshape(SIDE * SIDE * TOK, 128)
        pb[s] = lax.dot_general(h, d, (((0,), (0,)), ((), ())), preferred_element_type=F32)
    p_copy = send(pb.at[pl.ds((1 - core) * CAP, CAP)], pr, p_send.at[0], p_recv.at[0], partner)

    finish(0)
    turn(1)
    relay2(1)
    finish(1)
    p_copy.wait_recv()
    for k in range(CAP):
        present = slots[2, me * CAP + k].astype(F32)
        block_out[k] = ((pb[core * CAP + k] + pr[k]) * ((1.0 / 32.0) * present)).astype(BF)
    for copy in last:
        copy.wait_recv()
    for copy in started:
        copy.wait_send()


def shards(d_out, down_weight, gate_weight, up_weight, gate_pre, up_val, block_rows, block_cols, block_owner):
    vmem = pl.BlockSpec(memory_space=pltpu.VMEM)
    hbm = pl.BlockSpec(memory_space=pl.ANY)
    dma = pltpu.SemaphoreType.DMA
    grid_shape = (SIDE, SIDE, TOK)
    grad, blocks = pl.pallas_call(
        kernel,
        out_shape=(
            jax.ShapeDtypeStruct((TOK, WIDTH), BF),
            jax.ShapeDtypeStruct((CAP, 128, 128), BF),
        ),
        in_specs=[vmem] * 3 + [hbm] * 6,
        out_specs=(hbm, vmem),
        scratch_shapes=[
            pltpu.VMEM((WIN, WIDTH), BF),
            pltpu.VMEM((WIN, WIDTH), BF),
            pltpu.VMEM((WIN, WIDTH), BF),
            pltpu.VMEM((*grid_shape, WIDTH), BF),
            pltpu.VMEM((*grid_shape, WIN), BF),
            pltpu.VMEM((*grid_shape, WIN), BF),
            pltpu.VMEM((*grid_shape, WIN), BF),
            pltpu.VMEM((*grid_shape, WIDTH), BF),
            pltpu.VMEM((2, 6, SIDE, TOK, QUART), BF),
            pltpu.VMEM((2, 6, TOK, QUART), BF),
            pltpu.VMEM((TOK, WIDTH), BF),
            pltpu.VMEM((88, TOK, 128), BF),
            pltpu.VMEM((88, TOK, 128), BF),
            pltpu.VMEM((32, *grid_shape, 128), BF),
            pltpu.VMEM((16, 6, TOK, 128), BF),
            pltpu.VMEM((16, 6, TOK, 128), BF),
            pltpu.VMEM((6, 128, 128), F32),
            pltpu.VMEM((CAP, 128, 128), F32),
            pltpu.VMEM((8, 128), jnp.int32),
            pltpu.SMEM((8, 128), jnp.int32),
            dma((11,)),
            dma((3,)), dma((3,)),
            dma((2, 20)), dma((2, 20)),
            dma((2, 15)), dma((2, 15)),
            dma((15,)), dma((15,)),
            dma((2, 12)), dma((2, 12)),
            dma((2, 12)), dma((2, 12)),
            dma((2, 2)), dma((2, 2)),
            dma((1,)), dma((1,)),
        ],
        compiler_params=pltpu.CompilerParams(
            collective_id=0, has_side_effects=True, vmem_limit_bytes=62 * 1024 * 1024
        ),
        name="relay",
    )(block_rows, block_cols, block_owner, d_out[0], down_weight[0], gate_weight[0], up_weight[0], gate_pre[0], up_val[0])
    return (grad[None], blocks[None])


def solution(mesh):
    return jax.shard_map(
        shards,
        mesh=mesh,
        in_specs=(P("section", "dp", None),) * 6 + (P("section", None),) * 3,
        out_specs=(P("section", "dp", None), P("section", "dp", None, None)),
        check_vma=False,
    )
```

```python
import jax
import jax.numpy as jnp
from jax import lax
from jax.experimental import pallas as pl
from jax.experimental.pallas import tpu as pltpu
from jax.sharding import PartitionSpec as P

CAP = 3
MESH = pl.DeviceIdType.MESH
BF = jnp.bfloat16
F32 = jnp.float32
SIDE = 4
TOK = 48
WIDTH = 4096
UNITS = 352
WIN = 768
HALF = WIDTH // 2
QUART = WIDTH // 4
CHUNKS = ((0, 1024), (1024, 768), (1792, 256))
LAST = len(CHUNKS) - 1


def gelu_pair(values):
    coeff = 0.7978845608
    cubic = values * values * values
    tangent = jnp.tanh(coeff * (values + 0.044715 * cubic))
    activated = 0.5 * values * (1.0 + tangent)
    slope = 0.5 * (1.0 + tangent) + 0.5 * values * (1.0 - tangent * tangent) * coeff * (
        1.0 + 3.0 * 0.044715 * values * values
    )
    return (activated, slope)


def kernel(
    block_rows, block_cols, block_owner, d_out, w_down, w_gate, w_up, gate, up,
    grad_out, block_out,
    wd, wg, wu, x, gp, uq, lg, t, rb, rc, fin, gl, ul, xb, hs, hr, pb, pr, tab, slots,
    loc, w_send, w_recv, ag_send, ag_recv, a2_send, a2_recv, h_send, h_recv,
    rb_send, rb_recv, rc_send, rc_recv, x_send, x_recv, p_send, p_recv,
):
    sec = lax.axis_index("section")
    me = lax.axis_index("dp")
    core = lax.rem(me, 2)
    chip = lax.div(me, 2)
    yy = lax.div(chip, SIDE)
    zz = lax.rem(chip, SIDE)

    def dev(y, z):
        return (sec, (y * SIDE + z) * 2 + core)

    def step(p, by):
        return lax.rem(p + (by + SIDE), SIDE)

    partner = (sec, chip * 2 + (1 - core))
    prev_sec = (lax.rem(sec + 3, 4), me)
    next_sec = (lax.rem(sec + 1, 4), me)
    others = [(i, j) for i in range(SIDE) for j in range(SIDE) if (i, j) != (0, 0)]
    others.sort(key=lambda d: (2 not in d, -(min(d[0], SIDE - d[0]) + min(d[1], SIDE - d[1]))))
    n_far = sum(2 in d for d in others)

    barrier = pltpu.get_barrier_semaphore()
    for dy, dz in others:
        pl.semaphore_signal(barrier, inc=1, device_id=dev(step(yy, dy), step(zz, dz)), device_id_type=MESH)
    for target in (partner, prev_sec, next_sec):
        pl.semaphore_signal(barrier, inc=1, device_id=target, device_id_type=MESH)

    started = []

    def send(src, dst, s_sem, r_sem, target):
        copy = pltpu.make_async_remote_copy(
            src_ref=src, dst_ref=dst, send_sem=s_sem, recv_sem=r_sem,
            device_id=target, device_id_type=MESH,
        )
        copy.start()
        started.append(copy)
        return copy

    pad = 64 * lax.rem(chip, 2)
    place = pl.multiple_of(pad + core * UNITS, 32)
    rows = pl.ds(place, UNITS)
    local = [
        pltpu.make_async_copy(d_out, x.at[yy, zz], loc.at[0]),
        pltpu.make_async_copy(w_down, wd.at[rows], loc.at[3]),
        pltpu.make_async_copy(w_gate, wg.at[rows], loc.at[4]),
        pltpu.make_async_copy(w_up, wu.at[rows], loc.at[5]),
    ]
    for copy in local:
        copy.start()

    def lanes_of(k):
        return pl.ds(pl.multiple_of(k * 128, 128), 128)

    def load_block(k, carry):
        pltpu.make_async_copy(gate.at[:, lanes_of(k)], gl.at[k], loc.at[1]).start()
        pltpu.make_async_copy(up.at[:, lanes_of(k)], ul.at[k], loc.at[2]).start()
        return carry

    lax.fori_loop(0, gl.shape[0], load_block, 0)
    pl.semaphore_wait(barrier, len(others) + 3)

    def along(half, first, by, p, q):
        if (half == 0) == first:
            return dev(step(yy, by), zz)
        return dev(yy, step(zz, by))

    pos = [(yy, zz), (zz, yy)]

    def at(half, p, q):
        return (p, q) if half == 0 else (q, p)

    def cols(half, part=None):
        if part is None:
            return pl.ds(half * HALF, HALF)
        return pl.ds(half * HALF + part * QUART, QUART)

    def piece(half, p, q, part=None):
        a, b = at(half, p, q)
        return x.at[a, b, :, cols(half, part)]

    def ag(half, k, src, dst, target):
        return send(src, dst, ag_send.at[half, k], ag_recv.at[half, k], target)

    got = {}
    near = (0, -1, 1, 2)

    def spread(half, j, from_input=False):
        p, q = pos[half]
        pj = step(p, near[j])
        src = d_out.at[:, cols(half)] if from_input else piece(half, pj, q)
        dst = piece(half, pj, q)
        for n, by in ((0, 1), (1, -1)):
            got[half, 4 + 4 * j + n] = ag(half, 4 + 4 * j + n, src, dst, along(half, False, by, p, q))

    def pass_on(half, j):
        p, q = pos[half]
        pj = step(p, near[j])
        for n, by in ((0, 1), (1, -1)):
            got[half, 4 + 4 * j + n].wait_recv()
            ref = piece(half, pj, step(q, -by), n)
            got[half, 6 + 4 * j + n] = ag(half, 6 + 4 * j + n, ref, ref, along(half, False, by, p, q))

    for half in (0, 1):
        p, q = pos[half]
        for n, by in ((0, 1), (1, -1)):
            got[half, n] = ag(half, n, d_out.at[:, cols(half)], piece(half, p, q), along(half, True, by, p, q))
    w_copies = []
    for n, (src, dst) in enumerate(((w_down, wd), (w_gate, wg), (w_up, wu))):
        w_copies.append(send(src, dst.at[rows], w_send.at[n], w_recv.at[n], partner))
    for half in (0, 1):
        spread(half, 0, True)
    zero_rows = pl.ds(pl.multiple_of(704 - 11 * pad, 64), 64)
    for ref in (wd, wg, wu):
        ref[zero_rows, :] = jnp.zeros((64, WIDTH), BF)

    for n, by in ((0, 1), (1, -1)):
        for half in (0, 1):
            p, q = pos[half]
            got[half, n].wait_recv()
            ref = piece(half, step(p, -by), q, n)
            got[half, 2 + n] = ag(half, 2 + n, ref, ref, along(half, True, by, p, q))
        for half in (0, 1):
            spread(half, 1 + n)
    for half in (0, 1):
        pass_on(half, 0)

    blocks = block_owner.shape[1]
    row_id = lax.broadcasted_iota(jnp.int32, (blocks, blocks), 0)
    col_id = lax.broadcasted_iota(jnp.int32, (blocks, blocks), 1)

    def upright(ref):
        wide = jnp.broadcast_to(ref[...], (blocks, blocks))
        return jnp.sum(jnp.where(row_id == col_id, wide, 0), axis=1, keepdims=True)

    owner = upright(block_owner)
    earlier = (block_owner[...] == owner) & (col_id < row_id)
    position = owner * CAP + jnp.sum(jnp.where(earlier, 1, 0), axis=1, keepdims=True)
    match = position == lax.broadcasted_iota(jnp.int32, (blocks, 128), 1)
    for k, value in enumerate((upright(block_rows), upright(block_cols), jnp.ones((blocks, 1), jnp.int32))):
        tab[k : k + 1, :] = jnp.sum(jnp.where(match, value, 0), axis=0, keepdims=True)
    tables = pltpu.make_async_copy(tab, slots, loc.at[10])
    tables.start()
    tables.wait()

    pltpu.make_async_copy(gl, gl, loc.at[1]).wait()
    pltpu.make_async_copy(ul, ul, loc.at[2]).wait()

    def one_slot(s, carry):
        g = gl[slots[0, s]].astype(F32)
        u = ul[slots[0, s]].astype(F32)
        hs[lax.div(s, 6), lax.rem(s, 6)] = (gelu_pair(g)[0] * u).astype(BF)
        return carry

    lax.fori_loop(0, 48, one_slot, 0)
    for half in (0, 1):
        got[half, 2].wait_recv()
        got[half, 3].wait_recv()
        spread(half, 3)

    for half in (0, 1):
        pass_on(half, 1)
        pass_on(half, 2)
    lax.fori_loop(48, 96, one_slot, 0)
    for half in (0, 1):
        pass_on(half, 3)
    def window(g):
        return pl.ds(pl.multiple_of(lax.div(g * 11, 2) * 128, 128), WIN)

    a2 = []
    for some in (range(n_far), range(n_far, len(others))):
        for n, (src, dst) in enumerate(((gate, gp), (up, uq))):
            for k in some:
                ty, tz = step(yy, others[k][0]), step(zz, others[k][1])
                win = window(ty * SIDE + tz)
                a2.append(send(src.at[:, win], dst.at[yy, zz], a2_send.at[n, k], a2_recv.at[n, k], dev(ty, tz)))
    mine = window(chip)
    own = [
        pltpu.make_async_copy(gate.at[:, mine], gp.at[yy, zz], loc.at[6]),
        pltpu.make_async_copy(up.at[:, mine], uq.at[yy, zz], loc.at[7]),
    ]
    for copy in own:
        copy.start()
    hid = []

    def send_hidden(some):
        for k in some:
            ty, tz = step(yy, others[k][0]), step(zz, others[k][1])
            hid.append(send(hs.at[ty * SIDE + tz], hr.at[chip], h_send.at[k], h_recv.at[k], dev(ty, tz)))

    send_hidden(range(len(others)))
    own_h = pltpu.make_async_copy(hs.at[chip], hr.at[chip], loc.at[8])
    own_h.start()

    for j in range(4):
        for half in (0, 1):
            got[half, 6 + 4 * j].wait_recv()
            got[half, 7 + 4 * j].wait_recv()

    local[0].wait()

    def copy_block(k, carry):
        pltpu.make_async_copy(x.at[:, :, :, lanes_of(k)], xb.at[k], loc.at[9]).start()
        return carry

    lax.fori_loop(0, xb.shape[0], copy_block, 0)
    local[1].wait()
    w_copies[0].wait_recv()

    def dh_tile(i, carry):
        n = lax.div(i, 2)
        m = lax.rem(i, 2)
        units = pl.ds(pl.multiple_of(n * 256, 256), 256)
        a = x[pl.ds(m * 2, 2)].reshape(2 * SIDE * TOK, WIDTH)
        out = lax.dot_general(a, wd[units, :], (((1,), (1,)), ((), ())), preferred_element_type=F32)
        lg[pl.ds(m * 2, 2), :, :, units] = out.astype(BF).reshape(2, SIDE, TOK, 256)
        return carry

    lax.fori_loop(0, 6, dh_tile, 0)

    def point(a, b):
        for k in range(WIN // 128):
            lane = pl.ds(k * 128, 128)
            activated, slope = gelu_pair(gp[a, b, :, lane].astype(F32))
            dh = lg[a, b, :, lane].astype(F32)
            u = uq[a, b, :, lane].astype(F32)
            lg[a, b, :, lane] = (dh * u * slope).astype(BF)
            gp[a, b, :, lane] = (dh * activated).astype(BF)

    def near_of(i):
        return i + lax.div(i, 2)

    def point_y(i, carry):
        point(step(yy, 2), i)
        return carry

    def point_z(i, carry):
        point(step(yy, near_of(i)), step(zz, 2))
        return carry

    def point_near(i, carry):
        point(step(yy, near_of(lax.div(i, 3))), step(zz, near_of(lax.rem(i, 3))))
        return carry

    for copy in a2[: 2 * n_far]:
        copy.wait_recv()
    lax.fori_loop(0, SIDE, point_y, 0)
    lax.fori_loop(0, SIDE - 1, point_z, 0)
    for n in (2, 3):
        local[n].wait()
    for n in (1, 2):
        w_copies[n].wait_recv()

    def group(half, ref, p, lanes):
        if half == 0:
            return ref[p, :, :, lanes]
        return ref[:, p, :, lanes]

    def put(half, ref, p, lanes, value):
        if half == 0:
            ref[p, :, :, lanes] = value
        else:
            ref[:, p, :, lanes] = value

    def view(half, ref, p, lanes):
        if half == 0:
            return ref.at[p, :, :, lanes]
        return ref.at[:, p, :, lanes]

    def terms(half, c, targets):
        first, width = CHUNKS[c]

        def tile(i, carry):
            lanes = pl.ds(pl.multiple_of(half * HALF + first + i * 256, 256), 256)
            every = pl.ds(0, WIN)
            ga = jnp.concatenate([group(half, lg, p, every).reshape(SIDE * TOK, WIN) for p in targets], axis=0)
            ua = jnp.concatenate([group(half, gp, p, every).reshape(SIDE * TOK, WIN) for p in targets], axis=0)
            out = jnp.dot(ga, wg[:, lanes], preferred_element_type=F32)
            out = out + jnp.dot(ua, wu[:, lanes], preferred_element_type=F32)
            out = out.astype(BF)
            for k, p in enumerate(targets):
                part = out[k * SIDE * TOK : (k + 1) * SIDE * TOK]
                put(half, t, p, lanes, part.reshape(SIDE, TOK, 256))
            return carry

        lax.fori_loop(0, width // 256, tile, 0)

    def lanes_at(half, c, part):
        first, width = CHUNKS[c]
        return pl.ds(half * HALF + first + part * (width // 2), width // 2)

    def held(c):
        first, width = CHUNKS[c]
        return pl.ds(first // 2, width // 2)

    r1, r2 = {}, {}

    def rs1(half, c, k, by, part):
        p, q = pos[half]
        p_of = step(p, 2) if k < 2 else step(p, by)
        r1[half, c, k] = send(
            view(half, t, p_of, lanes_at(half, c, part)), rb.at[half, k, :, :, held(c)],
            rb_send.at[half, 6 * c + k], rb_recv.at[half, 6 * c + k], along(half, True, by, p, q),
        )

    def add_rows(half, c, dst_p, part, bufs):
        lanes = lanes_at(half, c, part)

        def row(i, carry):
            if half == 0:
                total = t[dst_p, i, :, lanes].astype(F32)
            else:
                total = t[i, dst_p, :, lanes].astype(F32)
            for k in bufs:
                total = total + rb[half, k, i, :, held(c)].astype(F32)
            if half == 0:
                t[dst_p, i, :, lanes] = total.astype(BF)
            else:
                t[i, dst_p, :, lanes] = total.astype(BF)
            return carry

        lax.fori_loop(0, SIDE, row, 0)

    def far(c):
        for half in (0, 1):
            terms(half, c, [step(pos[half][0], 2)])
            rs1(half, c, 0, 1, 0)
            rs1(half, c, 1, -1, 1)

    def near_terms(c):
        for half in (0, 1):
            p, q = pos[half]
            terms(half, c, [step(p, 1), step(p, -1)])
            rs1(half, c, 2, 1, 1)
            rs1(half, c, 3, -1, 0)

    def own_terms(c):
        for half in (0, 1):
            terms(half, c, [pos[half][0]])

    def relay(c):
        for k, by in ((0, 1), (1, -1)):
            for half in (0, 1):
                r1[half, c, k].wait_recv()
                add_rows(half, c, step(pos[half][0], by), k, (k,))
                rs1(half, c, 4 + k, by, k)

    def piece_t(half, c, q_of, part):
        a, b = at(half, pos[half][0], q_of)
        return (a, b, slice(None), lanes_at(half, c, part))

    def rs2(half, c, k, q_of, part, by):
        p, q = pos[half]
        r2[half, c, k] = send(
            t.at[piece_t(half, c, q_of, part)], rc.at[half, k, :, held(c)],
            rc_send.at[half, 6 * c + k], rc_recv.at[half, 6 * c + k], along(half, False, by, p, q),
        )

    def turn(c):
        for half in (0, 1):
            p, q = pos[half]
            for k in (2, 3, 4, 5):
                r1[half, c, k].wait_recv()
            add_rows(half, c, p, 0, (3, 4))
            add_rows(half, c, p, 1, (2, 5))
            if c == LAST:
                for part in (0, 1):
                    rs2(half, c, part, step(q, 2), part, 2)
                    rs2(half, c, 2 + part, step(q, 1), part, 1)
                    rs2(half, c, 4 + part, step(q, -1), part, -1)
                continue
            rs2(half, c, 0, step(q, 2), 0, 1)
            rs2(half, c, 1, step(q, 2), 1, -1)
            rs2(half, c, 2, step(q, 1), 1, 1)
            rs2(half, c, 3, step(q, -1), 0, -1)

    def relay2(c):
        for k, by in ((0, 1), (1, -1)):
            for half in (0, 1):
                q = pos[half][1]
                r2[half, c, k].wait_recv()
                here = piece_t(half, c, step(q, by), k)
                t[here] = (t[here].astype(F32) + rc[half, k, :, held(c)].astype(F32)).astype(BF)
                rs2(half, c, 4 + k, step(q, by), k, by)

    kept = jnp.minimum(sec, 1).astype(F32)
    last = []

    def finish(c):
        first, width = CHUNKS[c]
        for half in (0, 1):
            p, q = pos[half]
            for k in range(6) if c == LAST else (2, 3, 4, 5):
                r2[half, c, k].wait_recv()
            for part, bufs in ((0, (0, 2, 4)), (1, (1, 3, 5))) if c == LAST else ((0, (3, 4)), (1, (2, 5))):
                total = t[piece_t(half, c, q, part)].astype(F32)
                for k in bufs:
                    total = total + rc[half, k, :, held(c)].astype(F32)
                fin[:, lanes_at(half, c, part)] = (total * kept).astype(BF)
            lanes = pl.ds(half * HALF + first, width)
            last.append(send(
                fin.at[:, lanes], grad_out.at[:, lanes],
                x_send.at[half, c], x_recv.at[half, c], prev_sec,
            ))

    far(0)
    far(1)
    for copy in own:
        copy.wait()
    for copy in a2[2 * n_far :]:
        copy.wait_recv()
    lax.fori_loop(0, (SIDE - 1) * (SIDE - 1), point_near, 0)
    near_terms(0)
    relay(0)
    near_terms(1)
    own_terms(0)
    relay(1)
    own_terms(1)
    turn(0)
    own_terms(2)
    far(2)
    relay2(0)
    turn(1)
    near_terms(2)
    relay(2)

    own_h.wait()
    for copy in hid:
        copy.wait_recv()
    pltpu.make_async_copy(xb, xb, loc.at[9]).wait()
    for s in range(6):
        h = hr[:, s].reshape(SIDE * SIDE * TOK, 128)
        d = xb[slots[1, chip * 6 + s]].reshape(SIDE * SIDE * TOK, 128)
        pb[s] = lax.dot_general(h, d, (((0,), (0,)), ((), ())), preferred_element_type=F32)
    p_copy = send(pb.at[pl.ds((1 - core) * CAP, CAP)], pr, p_send.at[0], p_recv.at[0], partner)

    finish(0)
    relay2(1)
    turn(2)
    finish(1)
    finish(2)
    p_copy.wait_recv()
    for k in range(CAP):
        present = slots[2, me * CAP + k].astype(F32)
        block_out[k] = ((pb[core * CAP + k] + pr[k]) * ((1.0 / 32.0) * present)).astype(BF)
    for copy in last:
        copy.wait_recv()
    for copy in started:
        copy.wait_send()


def shards(d_out, down_weight, gate_weight, up_weight, gate_pre, up_val, block_rows, block_cols, block_owner):
    vmem = pl.BlockSpec(memory_space=pltpu.VMEM)
    hbm = pl.BlockSpec(memory_space=pl.ANY)
    dma = pltpu.SemaphoreType.DMA
    grid_shape = (SIDE, SIDE, TOK)
    grad, blocks = pl.pallas_call(
        kernel,
        out_shape=(
            jax.ShapeDtypeStruct((TOK, WIDTH), BF),
            jax.ShapeDtypeStruct((CAP, 128, 128), BF),
        ),
        in_specs=[vmem] * 3 + [hbm] * 6,
        out_specs=(hbm, vmem),
        scratch_shapes=[
            pltpu.VMEM((WIN, WIDTH), BF),
            pltpu.VMEM((WIN, WIDTH), BF),
            pltpu.VMEM((WIN, WIDTH), BF),
            pltpu.VMEM((*grid_shape, WIDTH), BF),
            pltpu.VMEM((*grid_shape, WIN), BF),
            pltpu.VMEM((*grid_shape, WIN), BF),
            pltpu.VMEM((*grid_shape, WIN), BF),
            pltpu.VMEM((*grid_shape, WIDTH), BF),
            pltpu.VMEM((2, 6, SIDE, TOK, QUART), BF),
            pltpu.VMEM((2, 6, TOK, QUART), BF),
            pltpu.VMEM((TOK, WIDTH), BF),
            pltpu.VMEM((88, TOK, 128), BF),
            pltpu.VMEM((88, TOK, 128), BF),
            pltpu.VMEM((32, *grid_shape, 128), BF),
            pltpu.VMEM((16, 6, TOK, 128), BF),
            pltpu.VMEM((16, 6, TOK, 128), BF),
            pltpu.VMEM((6, 128, 128), F32),
            pltpu.VMEM((CAP, 128, 128), F32),
            pltpu.VMEM((8, 128), jnp.int32),
            pltpu.SMEM((8, 128), jnp.int32),
            dma((11,)),
            dma((3,)), dma((3,)),
            dma((2, 20)), dma((2, 20)),
            dma((2, 15)), dma((2, 15)),
            dma((15,)), dma((15,)),
            dma((2, 18)), dma((2, 18)),
            dma((2, 18)), dma((2, 18)),
            dma((2, 3)), dma((2, 3)),
            dma((1,)), dma((1,)),
        ],
        compiler_params=pltpu.CompilerParams(
            collective_id=0, has_side_effects=True, vmem_limit_bytes=62 * 1024 * 1024
        ),
        name="relay",
    )(block_rows, block_cols, block_owner, d_out[0], down_weight[0], gate_weight[0], up_weight[0], gate_pre[0], up_val[0])
    return (grad[None], blocks[None])


def solution(mesh):
    return jax.shard_map(
        shards,
        mesh=mesh,
        in_specs=(P("section", "dp", None),) * 6 + (P("section", None),) * 3,
        out_specs=(P("section", "dp", None), P("section", "dp", None, None)),
        check_vma=False,
    )
```

```python
import jax
import jax.numpy as jnp
from jax import lax
from jax.experimental import pallas as pl
from jax.experimental.pallas import tpu as pltpu
from jax.sharding import PartitionSpec as P

CAP = 3
MESH = pl.DeviceIdType.MESH
BF = jnp.bfloat16
F32 = jnp.float32
SIDE = 4
TOK = 48
WIDTH = 4096
UNITS = 352
WIN = 768
HALF = WIDTH // 2
QUART = WIDTH // 4
CHUNKS = ((0, 1024), (1024, 768), (1792, 256))
LAST = len(CHUNKS) - 1


def gelu_pair(values):
    coeff = 0.7978845608
    cubic = values * values * values
    tangent = jnp.tanh(coeff * (values + 0.044715 * cubic))
    activated = 0.5 * values * (1.0 + tangent)
    slope = 0.5 * (1.0 + tangent) + 0.5 * values * (1.0 - tangent * tangent) * coeff * (
        1.0 + 3.0 * 0.044715 * values * values
    )
    return (activated, slope)


def kernel(
    block_rows, block_cols, block_owner, d_out, w_down, w_gate, w_up, gate, up,
    grad_out, block_out,
    wd, wg, wu, x, gp, uq, lg, t, rb, rc, fin, gl, ul, xb, hs, hr, pb, pr, tab, slots, done,
    loc, w_send, w_recv, ag_send, ag_recv, a2_send, a2_recv, h_send, h_recv,
    rb_send, rb_recv, rc_send, rc_recv, x_send, x_recv, p_send, p_recv,
):
    sec = lax.axis_index("section")
    me = lax.axis_index("dp")
    core = lax.rem(me, 2)
    chip = lax.div(me, 2)
    yy = lax.div(chip, SIDE)
    zz = lax.rem(chip, SIDE)

    def dev(y, z):
        return (sec, (y * SIDE + z) * 2 + core)

    def step(p, by):
        return lax.rem(p + (by + SIDE), SIDE)

    partner = (sec, chip * 2 + (1 - core))
    prev_sec = (lax.rem(sec + 3, 4), me)
    next_sec = (lax.rem(sec + 1, 4), me)
    others = [(i, j) for i in range(SIDE) for j in range(SIDE) if (i, j) != (0, 0)]
    others.sort(key=lambda d: (2 not in d, -(min(d[0], SIDE - d[0]) + min(d[1], SIDE - d[1]))))
    n_far = sum(2 in d for d in others)

    barrier = pltpu.get_barrier_semaphore()
    for dy, dz in others:
        pl.semaphore_signal(barrier, inc=1, device_id=dev(step(yy, dy), step(zz, dz)), device_id_type=MESH)
    for target in (partner, prev_sec, next_sec):
        pl.semaphore_signal(barrier, inc=1, device_id=target, device_id_type=MESH)

    started = []

    def send(src, dst, s_sem, r_sem, target):
        copy = pltpu.make_async_remote_copy(
            src_ref=src, dst_ref=dst, send_sem=s_sem, recv_sem=r_sem,
            device_id=target, device_id_type=MESH,
        )
        copy.start()
        started.append(copy)
        return copy

    pad = 64 * lax.rem(chip, 2)
    place = pl.multiple_of(pad + core * UNITS, 32)
    rows = pl.ds(place, UNITS)
    local = [
        pltpu.make_async_copy(d_out, x.at[yy, zz], loc.at[0]),
        pltpu.make_async_copy(w_down, wd.at[rows], loc.at[3]),
        pltpu.make_async_copy(w_gate, wg.at[rows], loc.at[4]),
        pltpu.make_async_copy(w_up, wu.at[rows], loc.at[5]),
    ]
    for copy in local:
        copy.start()

    def lanes_of(k):
        return pl.ds(pl.multiple_of(k * 128, 128), 128)

    def load_block(k, carry):
        pltpu.make_async_copy(gate.at[:, lanes_of(k)], gl.at[k], loc.at[1]).start()
        pltpu.make_async_copy(up.at[:, lanes_of(k)], ul.at[k], loc.at[2]).start()
        return carry

    lax.fori_loop(0, gl.shape[0], load_block, 0)
    pl.semaphore_wait(barrier, len(others) + 3)

    def along(half, first, by, p, q):
        if (half == 0) == first:
            return dev(step(yy, by), zz)
        return dev(yy, step(zz, by))

    pos = [(yy, zz), (zz, yy)]

    def at(half, p, q):
        return (p, q) if half == 0 else (q, p)

    def cols(half, part=None):
        if part is None:
            return pl.ds(half * HALF, HALF)
        return pl.ds(half * HALF + part * QUART, QUART)

    def piece(half, p, q, part=None):
        a, b = at(half, p, q)
        return x.at[a, b, :, cols(half, part)]

    def ag(half, k, src, dst, target):
        return send(src, dst, ag_send.at[half, k], ag_recv.at[half, k], target)

    got = {}
    near = (0, -1, 1, 2)

    def spread(half, j, from_input=False):
        p, q = pos[half]
        pj = step(p, near[j])
        src = d_out.at[:, cols(half)] if from_input else piece(half, pj, q)
        dst = piece(half, pj, q)
        for n, by in ((0, 1), (1, -1)):
            got[half, 4 + 4 * j + n] = ag(half, 4 + 4 * j + n, src, dst, along(half, False, by, p, q))

    def pass_on(half, j):
        p, q = pos[half]
        pj = step(p, near[j])
        for n, by in ((0, 1), (1, -1)):
            got[half, 4 + 4 * j + n].wait_recv()
            ref = piece(half, pj, step(q, -by), n)
            got[half, 6 + 4 * j + n] = ag(half, 6 + 4 * j + n, ref, ref, along(half, False, by, p, q))

    for half in (0, 1):
        p, q = pos[half]
        for n, by in ((0, 1), (1, -1)):
            got[half, n] = ag(half, n, d_out.at[:, cols(half)], piece(half, p, q), along(half, True, by, p, q))
    w_copies = []
    for n, (src, dst) in enumerate(((w_down, wd), (w_gate, wg), (w_up, wu))):
        w_copies.append(send(src, dst.at[rows], w_send.at[n], w_recv.at[n], partner))
    for half in (0, 1):
        spread(half, 0, True)
    zero_rows = pl.ds(pl.multiple_of(704 - 11 * pad, 64), 64)
    for ref in (wd, wg, wu):
        ref[zero_rows, :] = jnp.zeros((64, WIDTH), BF)

    for n, by in ((0, 1), (1, -1)):
        for half in (0, 1):
            p, q = pos[half]
            got[half, n].wait_recv()
            ref = piece(half, step(p, -by), q, n)
            got[half, 2 + n] = ag(half, 2 + n, ref, ref, along(half, True, by, p, q))
        for half in (0, 1):
            spread(half, 1 + n)
    for half in (0, 1):
        pass_on(half, 0)

    for half in (0, 1):
        got[half, 2].wait_recv()
        got[half, 3].wait_recv()
        spread(half, 3)

    for half in (0, 1):
        pass_on(half, 1)
        pass_on(half, 2)
    for half in (0, 1):
        pass_on(half, 3)
    def window(g):
        return pl.ds(pl.multiple_of(lax.div(g * 11, 2) * 128, 128), WIN)

    a2 = []
    for some in (range(n_far), range(n_far, len(others))):
        for n, (src, dst) in enumerate(((gate, gp), (up, uq))):
            for k in some:
                ty, tz = step(yy, others[k][0]), step(zz, others[k][1])
                win = window(ty * SIDE + tz)
                a2.append(send(src.at[:, win], dst.at[yy, zz], a2_send.at[n, k], a2_recv.at[n, k], dev(ty, tz)))
    mine = window(chip)
    own = [
        pltpu.make_async_copy(gate.at[:, mine], gp.at[yy, zz], loc.at[6]),
        pltpu.make_async_copy(up.at[:, mine], uq.at[yy, zz], loc.at[7]),
    ]
    for copy in own:
        copy.start()
    blocks = block_owner.shape[1]
    row_id = lax.broadcasted_iota(jnp.int32, (blocks, blocks), 0)
    col_id = lax.broadcasted_iota(jnp.int32, (blocks, blocks), 1)

    def upright(ref):
        wide = jnp.broadcast_to(ref[...], (blocks, blocks))
        return jnp.sum(jnp.where(row_id == col_id, wide, 0), axis=1, keepdims=True)

    owner = upright(block_owner)
    earlier = (block_owner[...] == owner) & (col_id < row_id)
    position = owner * CAP + jnp.sum(jnp.where(earlier, 1, 0), axis=1, keepdims=True)
    match = position == lax.broadcasted_iota(jnp.int32, (blocks, 128), 1)
    for k, value in enumerate((upright(block_rows), upright(block_cols), jnp.ones((blocks, 1), jnp.int32))):
        tab[k : k + 1, :] = jnp.sum(jnp.where(match, value, 0), axis=0, keepdims=True)
    tables = pltpu.make_async_copy(tab, slots, loc.at[10])
    tables.start()
    tables.wait()

    pltpu.make_async_copy(gl, gl, loc.at[1]).wait()
    pltpu.make_async_copy(ul, ul, loc.at[2]).wait()

    def one_slot(s, carry):
        g = gl[slots[0, s]].astype(F32)
        u = ul[slots[0, s]].astype(F32)
        hs[lax.div(s, 6), lax.rem(s, 6)] = (gelu_pair(g)[0] * u).astype(BF)
        return carry

    lax.fori_loop(0, 96, one_slot, 0)
    hid = []

    def send_hidden(some):
        for k in some:
            ty, tz = step(yy, others[k][0]), step(zz, others[k][1])
            hid.append(send(hs.at[ty * SIDE + tz], hr.at[chip], h_send.at[k], h_recv.at[k], dev(ty, tz)))

    send_hidden(range(len(others)))
    own_h = pltpu.make_async_copy(hs.at[chip], hr.at[chip], loc.at[8])
    own_h.start()

    for j in range(4):
        for half in (0, 1):
            got[half, 6 + 4 * j].wait_recv()
            got[half, 7 + 4 * j].wait_recv()

    local[0].wait()

    def copy_block(k, carry):
        pltpu.make_async_copy(x.at[:, :, :, lanes_of(k)], xb.at[k], loc.at[9]).start()
        return carry

    lax.fori_loop(0, xb.shape[0], copy_block, 0)
    local[1].wait()
    w_copies[0].wait_recv()

    def dh_tile(i, carry):
        n = lax.div(i, 2)
        m = lax.rem(i, 2)
        units = pl.ds(pl.multiple_of(n * 256, 256), 256)
        a = x[pl.ds(m * 2, 2)].reshape(2 * SIDE * TOK, WIDTH)
        out = lax.dot_general(a, wd[units, :], (((1,), (1,)), ((), ())), preferred_element_type=F32)
        lg[pl.ds(m * 2, 2), :, :, units] = out.astype(BF).reshape(2, SIDE, TOK, 256)
        return carry

    lax.fori_loop(0, 6, dh_tile, 0)

    def point(a, b):
        for k in range(WIN // 128):
            lane = pl.ds(k * 128, 128)
            activated, slope = gelu_pair(gp[a, b, :, lane].astype(F32))
            dh = lg[a, b, :, lane].astype(F32)
            u = uq[a, b, :, lane].astype(F32)
            lg[a, b, :, lane] = (dh * u * slope).astype(BF)
            gp[a, b, :, lane] = (dh * activated).astype(BF)

    def near_of(i):
        return i + lax.div(i, 2)

    def point_y(i, carry):
        point(step(yy, 2), i)
        return carry

    def point_z(i, carry):
        point(step(yy, near_of(i)), step(zz, 2))
        return carry

    def point_near(i, carry):
        point(step(yy, near_of(lax.div(i, 3))), step(zz, near_of(lax.rem(i, 3))))
        return carry

    for copy in a2[: 2 * n_far]:
        copy.wait_recv()
    lax.fori_loop(0, SIDE, point_y, 0)
    lax.fori_loop(0, SIDE - 1, point_z, 0)
    for n in (2, 3):
        local[n].wait()
    for n in (1, 2):
        w_copies[n].wait_recv()

    def group(half, ref, p, lanes):
        if half == 0:
            return ref[p, :, :, lanes]
        return ref[:, p, :, lanes]

    def put(half, ref, p, lanes, value):
        if half == 0:
            ref[p, :, :, lanes] = value
        else:
            ref[:, p, :, lanes] = value

    def view(half, ref, p, lanes):
        if half == 0:
            return ref.at[p, :, :, lanes]
        return ref.at[:, p, :, lanes]

    def terms(half, c, targets):
        first, width = CHUNKS[c]

        def tile(i, carry):
            lanes = pl.ds(pl.multiple_of(half * HALF + first + i * 256, 256), 256)
            every = pl.ds(0, WIN)
            ga = jnp.concatenate([group(half, lg, p, every).reshape(SIDE * TOK, WIN) for p in targets], axis=0)
            ua = jnp.concatenate([group(half, gp, p, every).reshape(SIDE * TOK, WIN) for p in targets], axis=0)
            out = jnp.dot(ga, wg[:, lanes], preferred_element_type=F32)
            out = out + jnp.dot(ua, wu[:, lanes], preferred_element_type=F32)
            out = out.astype(BF)
            for k, p in enumerate(targets):
                part = out[k * SIDE * TOK : (k + 1) * SIDE * TOK]
                put(half, t, p, lanes, part.reshape(SIDE, TOK, 256))
            return carry

        lax.fori_loop(0, width // 256, tile, 0)

    def lanes_at(half, c, part):
        first, width = CHUNKS[c]
        return pl.ds(half * HALF + first + part * (width // 2), width // 2)

    def held(c):
        first, width = CHUNKS[c]
        return pl.ds(first // 2, width // 2)

    r1, r2 = {}, {}

    def rs1(half, c, k, by, part):
        p, q = pos[half]
        p_of = step(p, 2) if k < 2 else step(p, by)
        r1[half, c, k] = send(
            view(half, t, p_of, lanes_at(half, c, part)), rb.at[half, k, :, :, held(c)],
            rb_send.at[half, 6 * c + k], rb_recv.at[half, 6 * c + k], along(half, True, by, p, q),
        )

    def add_rows(half, c, dst_p, part, bufs):
        lanes = lanes_at(half, c, part)

        def row(i, carry):
            if half == 0:
                total = t[dst_p, i, :, lanes].astype(F32)
            else:
                total = t[i, dst_p, :, lanes].astype(F32)
            for k in bufs:
                total = total + rb[half, k, i, :, held(c)].astype(F32)
            if half == 0:
                t[dst_p, i, :, lanes] = total.astype(BF)
            else:
                t[i, dst_p, :, lanes] = total.astype(BF)
            return carry

        lax.fori_loop(0, SIDE, row, 0)

    def far(c):
        for half in (0, 1):
            terms(half, c, [step(pos[half][0], 2)])
            rs1(half, c, 0, 1, 0)
            rs1(half, c, 1, -1, 1)

    def near_terms(c):
        for half in (0, 1):
            p, q = pos[half]
            terms(half, c, [step(p, 1), step(p, -1)])
            rs1(half, c, 2, 1, 1)
            rs1(half, c, 3, -1, 0)

    def own_terms(c):
        for half in (0, 1):
            terms(half, c, [pos[half][0]])

    def relay(c):
        for k, by in ((0, 1), (1, -1)):
            for half in (0, 1):
                r1[half, c, k].wait_recv()
                add_rows(half, c, step(pos[half][0], by), k, (k,))
                rs1(half, c, 4 + k, by, k)

    def piece_t(half, c, q_of, part):
        a, b = at(half, pos[half][0], q_of)
        return (a, b, slice(None), lanes_at(half, c, part))

    def rs2(half, c, k, q_of, part, by):
        p, q = pos[half]
        r2[half, c, k] = send(
            t.at[piece_t(half, c, q_of, part)], rc.at[half, k, :, held(c)],
            rc_send.at[half, 6 * c + k], rc_recv.at[half, 6 * c + k], along(half, False, by, p, q),
        )

    def turn(c):
        for half in (0, 1):
            p, q = pos[half]
            for k in (2, 3, 4, 5):
                r1[half, c, k].wait_recv()
            add_rows(half, c, p, 0, (3, 4))
            add_rows(half, c, p, 1, (2, 5))
            if c == LAST:
                for part in (0, 1):
                    rs2(half, c, part, step(q, 2), part, 2)
                    rs2(half, c, 2 + part, step(q, 1), part, 1)
                    rs2(half, c, 4 + part, step(q, -1), part, -1)
                continue
            rs2(half, c, 0, step(q, 2), 0, 1)
            rs2(half, c, 1, step(q, 2), 1, -1)
            rs2(half, c, 2, step(q, 1), 1, 1)
            rs2(half, c, 3, step(q, -1), 0, -1)

    def relay2(c):
        for k, by in ((0, 1), (1, -1)):
            for half in (0, 1):
                q = pos[half][1]
                r2[half, c, k].wait_recv()
                here = piece_t(half, c, step(q, by), k)
                t[here] = (t[here].astype(F32) + rc[half, k, :, held(c)].astype(F32)).astype(BF)
                rs2(half, c, 4 + k, step(q, by), k, by)

    kept = jnp.minimum(sec, 1).astype(F32)
    last = []

    def finish(c):
        first, width = CHUNKS[c]
        for half in (0, 1):
            p, q = pos[half]
            for k in range(6) if c == LAST else (2, 3, 4, 5):
                r2[half, c, k].wait_recv()
            for part, bufs in ((0, (0, 2, 4)), (1, (1, 3, 5))) if c == LAST else ((0, (3, 4)), (1, (2, 5))):
                total = t[piece_t(half, c, q, part)].astype(F32)
                for k in bufs:
                    total = total + rc[half, k, :, held(c)].astype(F32)
                fin[:, lanes_at(half, c, part)] = (total * kept).astype(BF)
            lanes = pl.ds(half * HALF + first, width)
            last.append(send(
                fin.at[:, lanes], grad_out.at[:, lanes],
                x_send.at[half, c], x_recv.at[half, c], prev_sec,
            ))

    far(0)
    far(1)
    for copy in own:
        copy.wait()
    for copy in a2[2 * n_far :]:
        copy.wait_recv()
    lax.fori_loop(0, (SIDE - 1) * (SIDE - 1), point_near, 0)
    near_terms(0)
    relay(0)
    near_terms(1)
    own_terms(0)
    relay(1)
    own_terms(1)
    turn(0)
    own_terms(2)
    far(2)
    relay2(0)
    turn(1)
    near_terms(2)
    relay(2)

    own_h.wait()
    for copy in hid:
        copy.wait_recv()
    pltpu.make_async_copy(xb, xb, loc.at[9]).wait()
    for s in range(6):
        h = hr[:, s].reshape(SIDE * SIDE * TOK, 128)
        d = xb[slots[1, chip * 6 + s]].reshape(SIDE * SIDE * TOK, 128)
        pb[s] = lax.dot_general(h, d, (((0,), (0,)), ((), ())), preferred_element_type=F32)
    p_copy = send(pb.at[pl.ds((1 - core) * CAP, CAP)], pr, p_send.at[0], p_recv.at[0], partner)

    finish(0)
    relay2(1)
    turn(2)
    finish(1)
    p_copy.wait_recv()
    for k in range(CAP):
        present = slots[2, me * CAP + k].astype(F32)
        done[k] = ((pb[core * CAP + k] + pr[k]) * ((1.0 / 32.0) * present)).astype(BF)
    done_copy = pltpu.make_async_copy(done, block_out, loc.at[11])
    done_copy.start()
    finish(2)
    done_copy.wait()
    for copy in last:
        copy.wait_recv()
    for copy in started:
        copy.wait_send()


def shards(d_out, down_weight, gate_weight, up_weight, gate_pre, up_val, block_rows, block_cols, block_owner):
    vmem = pl.BlockSpec(memory_space=pltpu.VMEM)
    hbm = pl.BlockSpec(memory_space=pl.ANY)
    dma = pltpu.SemaphoreType.DMA
    grid_shape = (SIDE, SIDE, TOK)
    grad, blocks = pl.pallas_call(
        kernel,
        out_shape=(
            jax.ShapeDtypeStruct((TOK, WIDTH), BF),
            jax.ShapeDtypeStruct((CAP, 128, 128), BF),
        ),
        in_specs=[vmem] * 3 + [hbm] * 6,
        out_specs=(hbm, hbm),
        scratch_shapes=[
            pltpu.VMEM((WIN, WIDTH), BF),
            pltpu.VMEM((WIN, WIDTH), BF),
            pltpu.VMEM((WIN, WIDTH), BF),
            pltpu.VMEM((*grid_shape, WIDTH), BF),
            pltpu.VMEM((*grid_shape, WIN), BF),
            pltpu.VMEM((*grid_shape, WIN), BF),
            pltpu.VMEM((*grid_shape, WIN), BF),
            pltpu.VMEM((*grid_shape, WIDTH), BF),
            pltpu.VMEM((2, 6, SIDE, TOK, QUART), BF),
            pltpu.VMEM((2, 6, TOK, QUART), BF),
            pltpu.VMEM((TOK, WIDTH), BF),
            pltpu.VMEM((88, TOK, 128), BF),
            pltpu.VMEM((88, TOK, 128), BF),
            pltpu.VMEM((32, *grid_shape, 128), BF),
            pltpu.VMEM((16, 6, TOK, 128), BF),
            pltpu.VMEM((16, 6, TOK, 128), BF),
            pltpu.VMEM((6, 128, 128), F32),
            pltpu.VMEM((CAP, 128, 128), F32),
            pltpu.VMEM((8, 128), jnp.int32),
            pltpu.SMEM((8, 128), jnp.int32),
            pltpu.VMEM((CAP, 128, 128), BF),
            dma((12,)),
            dma((3,)), dma((3,)),
            dma((2, 20)), dma((2, 20)),
            dma((2, 15)), dma((2, 15)),
            dma((15,)), dma((15,)),
            dma((2, 18)), dma((2, 18)),
            dma((2, 18)), dma((2, 18)),
            dma((2, 3)), dma((2, 3)),
            dma((1,)), dma((1,)),
        ],
        compiler_params=pltpu.CompilerParams(
            collective_id=0, has_side_effects=True, vmem_limit_bytes=62 * 1024 * 1024
        ),
        name="relay",
    )(block_rows, block_cols, block_owner, d_out[0], down_weight[0], gate_weight[0], up_weight[0], gate_pre[0], up_val[0])
    return (grad[None], blocks[None])


def solution(mesh):
    return jax.shard_map(
        shards,
        mesh=mesh,
        in_specs=(P("section", "dp", None),) * 6 + (P("section", None),) * 3,
        out_specs=(P("section", "dp", None), P("section", "dp", None, None)),
        check_vma=False,
    )
```

```python
import jax
import jax.numpy as jnp
from jax import lax
from jax.experimental import pallas as pl
from jax.experimental.pallas import tpu as pltpu
from jax.sharding import PartitionSpec as P

CAP = 3
MESH = pl.DeviceIdType.MESH
BF = jnp.bfloat16
F32 = jnp.float32
SIDE = 4
TOK = 48
WIDTH = 4096
UNITS = 352
WIN = 768
HALF = WIDTH // 2
QUART = WIDTH // 4
CHUNKS = ((0, 1280), (1280, 512), (1792, 256))
LAST = len(CHUNKS) - 1


def gelu_pair(values):
    coeff = 0.7978845608
    cubic = values * values * values
    tangent = jnp.tanh(coeff * (values + 0.044715 * cubic))
    activated = 0.5 * values * (1.0 + tangent)
    slope = 0.5 * (1.0 + tangent) + 0.5 * values * (1.0 - tangent * tangent) * coeff * (
        1.0 + 3.0 * 0.044715 * values * values
    )
    return (activated, slope)


def kernel(
    block_rows, block_cols, block_owner, d_out, w_down, w_gate, w_up, gate, up,
    grad_out, block_out,
    wd, wg, wu, x, gp, uq, lg, t, rb, rc, fin, gl, ul, xb, hs, hr, pb, pr, tab, slots, done,
    loc, w_send, w_recv, ag_send, ag_recv, a2_send, a2_recv, h_send, h_recv,
    rb_send, rb_recv, rc_send, rc_recv, x_send, x_recv, p_send, p_recv,
):
    sec = lax.axis_index("section")
    me = lax.axis_index("dp")
    core = lax.rem(me, 2)
    chip = lax.div(me, 2)
    yy = lax.div(chip, SIDE)
    zz = lax.rem(chip, SIDE)

    def dev(y, z):
        return (sec, (y * SIDE + z) * 2 + core)

    def step(p, by):
        return lax.rem(p + (by + SIDE), SIDE)

    partner = (sec, chip * 2 + (1 - core))
    prev_sec = (lax.rem(sec + 3, 4), me)
    next_sec = (lax.rem(sec + 1, 4), me)
    others = [(i, j) for i in range(SIDE) for j in range(SIDE) if (i, j) != (0, 0)]
    others.sort(key=lambda d: (2 not in d, -(min(d[0], SIDE - d[0]) + min(d[1], SIDE - d[1]))))
    n_far = sum(2 in d for d in others)

    barrier = pltpu.get_barrier_semaphore()
    for dy, dz in others:
        pl.semaphore_signal(barrier, inc=1, device_id=dev(step(yy, dy), step(zz, dz)), device_id_type=MESH)
    for target in (partner, prev_sec, next_sec):
        pl.semaphore_signal(barrier, inc=1, device_id=target, device_id_type=MESH)

    started = []

    def send(src, dst, s_sem, r_sem, target):
        copy = pltpu.make_async_remote_copy(
            src_ref=src, dst_ref=dst, send_sem=s_sem, recv_sem=r_sem,
            device_id=target, device_id_type=MESH,
        )
        copy.start()
        started.append(copy)
        return copy

    pad = 64 * lax.rem(chip, 2)
    place = pl.multiple_of(pad + core * UNITS, 32)
    rows = pl.ds(place, UNITS)
    local = [
        pltpu.make_async_copy(d_out, x.at[yy, zz], loc.at[0]),
        pltpu.make_async_copy(w_down, wd.at[rows], loc.at[3]),
        pltpu.make_async_copy(w_gate, wg.at[rows], loc.at[4]),
        pltpu.make_async_copy(w_up, wu.at[rows], loc.at[5]),
    ]
    for copy in local:
        copy.start()

    def lanes_of(k):
        return pl.ds(pl.multiple_of(k * 128, 128), 128)

    def load_block(k, carry):
        pltpu.make_async_copy(gate.at[:, lanes_of(k)], gl.at[k], loc.at[1]).start()
        pltpu.make_async_copy(up.at[:, lanes_of(k)], ul.at[k], loc.at[2]).start()
        return carry

    lax.fori_loop(0, gl.shape[0], load_block, 0)
    pl.semaphore_wait(barrier, len(others) + 3)

    def along(half, first, by, p, q):
        if (half == 0) == first:
            return dev(step(yy, by), zz)
        return dev(yy, step(zz, by))

    pos = [(yy, zz), (zz, yy)]

    def at(half, p, q):
        return (p, q) if half == 0 else (q, p)

    def cols(half, part=None):
        if part is None:
            return pl.ds(half * HALF, HALF)
        return pl.ds(half * HALF + part * QUART, QUART)

    def piece(half, p, q, part=None):
        a, b = at(half, p, q)
        return x.at[a, b, :, cols(half, part)]

    def ag(half, k, src, dst, target):
        return send(src, dst, ag_send.at[half, k], ag_recv.at[half, k], target)

    got = {}
    near = (0, -1, 1, 2)

    def spread(half, j, from_input=False):
        p, q = pos[half]
        pj = step(p, near[j])
        src = d_out.at[:, cols(half)] if from_input else piece(half, pj, q)
        dst = piece(half, pj, q)
        for n, by in ((0, 1), (1, -1)):
            got[half, 4 + 4 * j + n] = ag(half, 4 + 4 * j + n, src, dst, along(half, False, by, p, q))

    def pass_on(half, j):
        p, q = pos[half]
        pj = step(p, near[j])
        for n, by in ((0, 1), (1, -1)):
            got[half, 4 + 4 * j + n].wait_recv()
            ref = piece(half, pj, step(q, -by), n)
            got[half, 6 + 4 * j + n] = ag(half, 6 + 4 * j + n, ref, ref, along(half, False, by, p, q))

    for half in (0, 1):
        p, q = pos[half]
        for n, by in ((0, 1), (1, -1)):
            got[half, n] = ag(half, n, d_out.at[:, cols(half)], piece(half, p, q), along(half, True, by, p, q))
    w_copies = []
    for n, (src, dst) in enumerate(((w_down, wd), (w_gate, wg), (w_up, wu))):
        w_copies.append(send(src, dst.at[rows], w_send.at[n], w_recv.at[n], partner))
    for half in (0, 1):
        spread(half, 0, True)
    zero_rows = pl.ds(pl.multiple_of(704 - 11 * pad, 64), 64)
    for ref in (wd, wg, wu):
        ref[zero_rows, :] = jnp.zeros((64, WIDTH), BF)

    for n, by in ((0, 1), (1, -1)):
        for half in (0, 1):
            p, q = pos[half]
            got[half, n].wait_recv()
            ref = piece(half, step(p, -by), q, n)
            got[half, 2 + n] = ag(half, 2 + n, ref, ref, along(half, True, by, p, q))
        for half in (0, 1):
            spread(half, 1 + n)
    for half in (0, 1):
        pass_on(half, 0)

    for half in (0, 1):
        got[half, 2].wait_recv()
        got[half, 3].wait_recv()
        spread(half, 3)

    for half in (0, 1):
        pass_on(half, 1)
        pass_on(half, 2)
    for half in (0, 1):
        pass_on(half, 3)
    def window(g):
        return pl.ds(pl.multiple_of(lax.div(g * 11, 2) * 128, 128), WIN)

    a2 = []
    for some in (range(n_far), range(n_far, len(others))):
        for n, (src, dst) in enumerate(((gate, gp), (up, uq))):
            for k in some:
                ty, tz = step(yy, others[k][0]), step(zz, others[k][1])
                win = window(ty * SIDE + tz)
                a2.append(send(src.at[:, win], dst.at[yy, zz], a2_send.at[n, k], a2_recv.at[n, k], dev(ty, tz)))
    mine = window(chip)
    own = [
        pltpu.make_async_copy(gate.at[:, mine], gp.at[yy, zz], loc.at[6]),
        pltpu.make_async_copy(up.at[:, mine], uq.at[yy, zz], loc.at[7]),
    ]
    for copy in own:
        copy.start()
    blocks = block_owner.shape[1]
    row_id = lax.broadcasted_iota(jnp.int32, (blocks, blocks), 0)
    col_id = lax.broadcasted_iota(jnp.int32, (blocks, blocks), 1)

    def upright(ref):
        wide = jnp.broadcast_to(ref[...], (blocks, blocks))
        return jnp.sum(jnp.where(row_id == col_id, wide, 0), axis=1, keepdims=True)

    owner = upright(block_owner)
    earlier = (block_owner[...] == owner) & (col_id < row_id)
    position = owner * CAP + jnp.sum(jnp.where(earlier, 1, 0), axis=1, keepdims=True)
    match = position == lax.broadcasted_iota(jnp.int32, (blocks, 128), 1)
    for k, value in enumerate((upright(block_rows), upright(block_cols), jnp.ones((blocks, 1), jnp.int32))):
        tab[k : k + 1, :] = jnp.sum(jnp.where(match, value, 0), axis=0, keepdims=True)
    tables = pltpu.make_async_copy(tab, slots, loc.at[10])
    tables.start()
    tables.wait()

    pltpu.make_async_copy(gl, gl, loc.at[1]).wait()
    pltpu.make_async_copy(ul, ul, loc.at[2]).wait()

    def one_slot(s, carry):
        g = gl[slots[0, s]].astype(F32)
        u = ul[slots[0, s]].astype(F32)
        hs[lax.div(s, 6), lax.rem(s, 6)] = (gelu_pair(g)[0] * u).astype(BF)
        return carry

    lax.fori_loop(0, 96, one_slot, 0)
    hid = []

    def send_hidden(some):
        for k in some:
            ty, tz = step(yy, others[k][0]), step(zz, others[k][1])
            hid.append(send(hs.at[ty * SIDE + tz], hr.at[chip], h_send.at[k], h_recv.at[k], dev(ty, tz)))

    send_hidden(range(len(others)))
    own_h = pltpu.make_async_copy(hs.at[chip], hr.at[chip], loc.at[8])
    own_h.start()

    for j in range(4):
        for half in (0, 1):
            got[half, 6 + 4 * j].wait_recv()
            got[half, 7 + 4 * j].wait_recv()

    local[0].wait()

    def copy_block(k, carry):
        pltpu.make_async_copy(x.at[:, :, :, lanes_of(k)], xb.at[k], loc.at[9]).start()
        return carry

    lax.fori_loop(0, xb.shape[0], copy_block, 0)
    local[1].wait()
    w_copies[0].wait_recv()

    def dh_tile(i, carry):
        n = lax.div(i, 2)
        m = lax.rem(i, 2)
        units = pl.ds(pl.multiple_of(n * 256, 256), 256)
        a = x[pl.ds(m * 2, 2)].reshape(2 * SIDE * TOK, WIDTH)
        out = lax.dot_general(a, wd[units, :], (((1,), (1,)), ((), ())), preferred_element_type=F32)
        lg[pl.ds(m * 2, 2), :, :, units] = out.astype(BF).reshape(2, SIDE, TOK, 256)
        return carry

    lax.fori_loop(0, 6, dh_tile, 0)

    def point(a, b):
        for k in range(WIN // 128):
            lane = pl.ds(k * 128, 128)
            activated, slope = gelu_pair(gp[a, b, :, lane].astype(F32))
            dh = lg[a, b, :, lane].astype(F32)
            u = uq[a, b, :, lane].astype(F32)
            lg[a, b, :, lane] = (dh * u * slope).astype(BF)
            gp[a, b, :, lane] = (dh * activated).astype(BF)

    def near_of(i):
        return i + lax.div(i, 2)

    def point_y(i, carry):
        point(step(yy, 2), i)
        return carry

    def point_z(i, carry):
        point(step(yy, near_of(i)), step(zz, 2))
        return carry

    def point_near(i, carry):
        point(step(yy, near_of(lax.div(i, 3))), step(zz, near_of(lax.rem(i, 3))))
        return carry

    for copy in a2[: 2 * n_far]:
        copy.wait_recv()
    lax.fori_loop(0, SIDE, point_y, 0)
    lax.fori_loop(0, SIDE - 1, point_z, 0)
    for n in (2, 3):
        local[n].wait()
    for n in (1, 2):
        w_copies[n].wait_recv()

    def group(half, ref, p, lanes):
        if half == 0:
            return ref[p, :, :, lanes]
        return ref[:, p, :, lanes]

    def put(half, ref, p, lanes, value):
        if half == 0:
            ref[p, :, :, lanes] = value
        else:
            ref[:, p, :, lanes] = value

    def view(half, ref, p, lanes):
        if half == 0:
            return ref.at[p, :, :, lanes]
        return ref.at[:, p, :, lanes]

    def terms(half, c, targets):
        first, width = CHUNKS[c]

        def tile(i, carry):
            lanes = pl.ds(pl.multiple_of(half * HALF + first + i * 256, 256), 256)
            every = pl.ds(0, WIN)
            ga = jnp.concatenate([group(half, lg, p, every).reshape(SIDE * TOK, WIN) for p in targets], axis=0)
            ua = jnp.concatenate([group(half, gp, p, every).reshape(SIDE * TOK, WIN) for p in targets], axis=0)
            out = jnp.dot(ga, wg[:, lanes], preferred_element_type=F32)
            out = out + jnp.dot(ua, wu[:, lanes], preferred_element_type=F32)
            out = out.astype(BF)
            for k, p in enumerate(targets):
                part = out[k * SIDE * TOK : (k + 1) * SIDE * TOK]
                put(half, t, p, lanes, part.reshape(SIDE, TOK, 256))
            return carry

        lax.fori_loop(0, width // 256, tile, 0)

    def lanes_at(half, c, part):
        first, width = CHUNKS[c]
        return pl.ds(half * HALF + first + part * (width // 2), width // 2)

    def held(c):
        first, width = CHUNKS[c]
        return pl.ds(first // 2, width // 2)

    r1, r2 = {}, {}

    def rs1(half, c, k, by, part):
        p, q = pos[half]
        p_of = step(p, 2) if k < 2 else step(p, by)
        r1[half, c, k] = send(
            view(half, t, p_of, lanes_at(half, c, part)), rb.at[half, k, :, :, held(c)],
            rb_send.at[half, 6 * c + k], rb_recv.at[half, 6 * c + k], along(half, True, by, p, q),
        )

    def add_rows(half, c, dst_p, part, bufs):
        lanes = lanes_at(half, c, part)

        def row(i, carry):
            if half == 0:
                total = t[dst_p, i, :, lanes].astype(F32)
            else:
                total = t[i, dst_p, :, lanes].astype(F32)
            for k in bufs:
                total = total + rb[half, k, i, :, held(c)].astype(F32)
            if half == 0:
                t[dst_p, i, :, lanes] = total.astype(BF)
            else:
                t[i, dst_p, :, lanes] = total.astype(BF)
            return carry

        lax.fori_loop(0, SIDE, row, 0)

    def far(c):
        for half in (0, 1):
            terms(half, c, [step(pos[half][0], 2)])
            rs1(half, c, 0, 1, 0)
            rs1(half, c, 1, -1, 1)

    def near_terms(c):
        for half in (0, 1):
            p, q = pos[half]
            terms(half, c, [step(p, 1), step(p, -1)])
            rs1(half, c, 2, 1, 1)
            rs1(half, c, 3, -1, 0)

    def own_terms(c):
        for half in (0, 1):
            terms(half, c, [pos[half][0]])

    def relay(c):
        for k, by in ((0, 1), (1, -1)):
            for half in (0, 1):
                r1[half, c, k].wait_recv()
                add_rows(half, c, step(pos[half][0], by), k, (k,))
                rs1(half, c, 4 + k, by, k)

    def piece_t(half, c, q_of, part):
        a, b = at(half, pos[half][0], q_of)
        return (a, b, slice(None), lanes_at(half, c, part))

    def rs2(half, c, k, q_of, part, by):
        p, q = pos[half]
        r2[half, c, k] = send(
            t.at[piece_t(half, c, q_of, part)], rc.at[half, k, :, held(c)],
            rc_send.at[half, 6 * c + k], rc_recv.at[half, 6 * c + k], along(half, False, by, p, q),
        )

    def turn(c):
        for half in (0, 1):
            p, q = pos[half]
            for k in (2, 3, 4, 5):
                r1[half, c, k].wait_recv()
            add_rows(half, c, p, 0, (3, 4))
            add_rows(half, c, p, 1, (2, 5))
            if c == LAST:
                for part in (0, 1):
                    rs2(half, c, part, step(q, 2), part, 2)
                    rs2(half, c, 2 + part, step(q, 1), part, 1)
                    rs2(half, c, 4 + part, step(q, -1), part, -1)
                continue
            rs2(half, c, 0, step(q, 2), 0, 1)
            rs2(half, c, 1, step(q, 2), 1, -1)
            rs2(half, c, 2, step(q, 1), 1, 1)
            rs2(half, c, 3, step(q, -1), 0, -1)

    def relay2(c):
        for k, by in ((0, 1), (1, -1)):
            for half in (0, 1):
                q = pos[half][1]
                r2[half, c, k].wait_recv()
                here = piece_t(half, c, step(q, by), k)
                t[here] = (t[here].astype(F32) + rc[half, k, :, held(c)].astype(F32)).astype(BF)
                rs2(half, c, 4 + k, step(q, by), k, by)

    kept = jnp.minimum(sec, 1).astype(F32)
    last = []

    def finish(c):
        first, width = CHUNKS[c]
        for half in (0, 1):
            p, q = pos[half]
            for k in range(6) if c == LAST else (2, 3, 4, 5):
                r2[half, c, k].wait_recv()
            for part, bufs in ((0, (0, 2, 4)), (1, (1, 3, 5))) if c == LAST else ((0, (3, 4)), (1, (2, 5))):
                total = t[piece_t(half, c, q, part)].astype(F32)
                for k in bufs:
                    total = total + rc[half, k, :, held(c)].astype(F32)
                fin[:, lanes_at(half, c, part)] = (total * kept).astype(BF)
            lanes = pl.ds(half * HALF + first, width)
            last.append(send(
                fin.at[:, lanes], grad_out.at[:, lanes],
                x_send.at[half, c], x_recv.at[half, c], prev_sec,
            ))

    far(0)
    far(1)
    for copy in own:
        copy.wait()
    for copy in a2[2 * n_far :]:
        copy.wait_recv()
    lax.fori_loop(0, (SIDE - 1) * (SIDE - 1), point_near, 0)
    near_terms(0)
    relay(0)
    near_terms(1)
    own_terms(0)
    relay(1)
    own_terms(1)
    turn(0)
    own_terms(2)
    far(2)
    relay2(0)
    turn(1)
    near_terms(2)
    relay(2)

    own_h.wait()
    for copy in hid:
        copy.wait_recv()
    pltpu.make_async_copy(xb, xb, loc.at[9]).wait()
    for s in range(6):
        h = hr[:, s].reshape(SIDE * SIDE * TOK, 128)
        d = xb[slots[1, chip * 6 + s]].reshape(SIDE * SIDE * TOK, 128)
        pb[s] = lax.dot_general(h, d, (((0,), (0,)), ((), ())), preferred_element_type=F32)
    p_copy = send(pb.at[pl.ds((1 - core) * CAP, CAP)], pr, p_send.at[0], p_recv.at[0], partner)

    finish(0)
    relay2(1)
    turn(2)
    finish(1)
    p_copy.wait_recv()
    for k in range(CAP):
        present = slots[2, me * CAP + k].astype(F32)
        done[k] = ((pb[core * CAP + k] + pr[k]) * ((1.0 / 32.0) * present)).astype(BF)
    done_copy = pltpu.make_async_copy(done, block_out, loc.at[11])
    done_copy.start()
    finish(2)
    done_copy.wait()
    for copy in last:
        copy.wait_recv()
    for copy in started:
        copy.wait_send()


def shards(d_out, down_weight, gate_weight, up_weight, gate_pre, up_val, block_rows, block_cols, block_owner):
    vmem = pl.BlockSpec(memory_space=pltpu.VMEM)
    hbm = pl.BlockSpec(memory_space=pl.ANY)
    dma = pltpu.SemaphoreType.DMA
    grid_shape = (SIDE, SIDE, TOK)
    grad, blocks = pl.pallas_call(
        kernel,
        out_shape=(
            jax.ShapeDtypeStruct((TOK, WIDTH), BF),
            jax.ShapeDtypeStruct((CAP, 128, 128), BF),
        ),
        in_specs=[vmem] * 3 + [hbm] * 6,
        out_specs=(hbm, hbm),
        scratch_shapes=[
            pltpu.VMEM((WIN, WIDTH), BF),
            pltpu.VMEM((WIN, WIDTH), BF),
            pltpu.VMEM((WIN, WIDTH), BF),
            pltpu.VMEM((*grid_shape, WIDTH), BF),
            pltpu.VMEM((*grid_shape, WIN), BF),
            pltpu.VMEM((*grid_shape, WIN), BF),
            pltpu.VMEM((*grid_shape, WIN), BF),
            pltpu.VMEM((*grid_shape, WIDTH), BF),
            pltpu.VMEM((2, 6, SIDE, TOK, QUART), BF),
            pltpu.VMEM((2, 6, TOK, QUART), BF),
            pltpu.VMEM((TOK, WIDTH), BF),
            pltpu.VMEM((88, TOK, 128), BF),
            pltpu.VMEM((88, TOK, 128), BF),
            pltpu.VMEM((32, *grid_shape, 128), BF),
            pltpu.VMEM((16, 6, TOK, 128), BF),
            pltpu.VMEM((16, 6, TOK, 128), BF),
            pltpu.VMEM((6, 128, 128), F32),
            pltpu.VMEM((CAP, 128, 128), F32),
            pltpu.VMEM((8, 128), jnp.int32),
            pltpu.SMEM((8, 128), jnp.int32),
            pltpu.VMEM((CAP, 128, 128), BF),
            dma((12,)),
            dma((3,)), dma((3,)),
            dma((2, 20)), dma((2, 20)),
            dma((2, 15)), dma((2, 15)),
            dma((15,)), dma((15,)),
            dma((2, 18)), dma((2, 18)),
            dma((2, 18)), dma((2, 18)),
            dma((2, 3)), dma((2, 3)),
            dma((1,)), dma((1,)),
        ],
        compiler_params=pltpu.CompilerParams(
            collective_id=0, has_side_effects=True, vmem_limit_bytes=62 * 1024 * 1024
        ),
        name="relay",
    )(block_rows, block_cols, block_owner, d_out[0], down_weight[0], gate_weight[0], up_weight[0], gate_pre[0], up_val[0])
    return (grad[None], blocks[None])


def solution(mesh):
    return jax.shard_map(
        shards,
        mesh=mesh,
        in_specs=(P("section", "dp", None),) * 6 + (P("section", None),) * 3,
        out_specs=(P("section", "dp", None), P("section", "dp", None, None)),
        check_vma=False,
    )
```
